32 devices in a mesh: batch: 4 (over y, core), seq: 8 (over z, x).
Axes of the slice: x: 2, y: 2, z: 4, core: 2. Of those that a mesh axis runs over, the one named last changes fastest.
Arguments:
- hidden_in: bfloat16 [8, 1024, 2560], P('batch', 'seq'), may hold values from -40 to 40
- attn_gain: bfloat16 [2560], P(('batch', 'seq')), may hold values from 0.25 to 1.75
- query_weight: bfloat16 [2560, 2560], P(('batch', 'seq')), may hold values from -0.125 to 0.125
- key_weight: bfloat16 [2560, 640], P(('batch', 'seq')), may hold values from -0.125 to 0.125
- value_weight: bfloat16 [2560, 640], P(('batch', 'seq')), may hold values from -0.125 to 0.125
- out_weight: bfloat16 [2560, 2560], P(('batch', 'seq')), may hold values from -0.625 to 0.625
- mlp_gain: bfloat16 [2560], P(('batch', 'seq')), may hold values from 0.25 to 1.75
- gate_weight: bfloat16 [2560, 6912], P(('batch', 'seq')), may hold values from -0.125 to 0.125
- up_weight: bfloat16 [2560, 6912], P(('batch', 'seq')), may hold values from -0.125 to 0.125
- down_weight: bfloat16 [2560, 6912], P(('batch', 'seq')), may hold values from -0.078125 to 0.078125
- segment_ids: int32 [8, 1024], P('batch'), may hold values from 0 to 127, as said below
- grad_output: bfloat16 [8, 1024, 2560], P('batch', 'seq'), may hold values from -6 to 6
Outputs:
- output: bfloat16 [8, 1024, 2560], P('batch', 'seq')
- grad_input: float32 [8, 1024, 2560], P('batch', 'seq')
- grad_attn_gain: float32 [2560], P(('batch', 'seq'))
- grad_query: float32 [2560, 2560], P(('batch', 'seq'))
- grad_key: float32 [2560, 640], P(('batch', 'seq'))
- grad_value: float32 [2560, 640], P(('batch', 'seq'))
- grad_out: float32 [2560, 2560], P(('batch', 'seq'))
- grad_mlp_gain: float32 [2560], P(('batch', 'seq'))
- grad_gate: float32 [2560, 6912], P(('batch', 'seq'))
- grad_up: float32 [2560, 6912], P(('batch', 'seq'))
- grad_down: float32 [2560, 6912], P(('batch', 'seq'))
The draws below stay inside these ranges and needn't reach their ends.
Inputs may be any that keep to these rules, and one draw needn't show every extreme that they name: `segment_ids`: in each sequence the ids start at 0, never fall, rise by at most one from a token to the next and rise only at positions that are multiples of 8; among the 2 sequences of each index of batch one is a single document; some sequence starts a new document at every multiple of 8.
All inputs are finite; a program needn't handle non-finite values.
Results may differ from the reference program's by a relative error of at most 0.013.
Values may be sent and summed in bfloat16 or wider, within the bound.
A program may use at most 896 MiB of HBM per device.

```python
import math
import jax
import jax.numpy as jnp
from jax import lax

D = 2560
HEADS = 32
KV_HEADS = 8
HEAD_DIM = 80
FF = 6912
SEQ_LEN = 1024
SEQ_B = 2
SEQS = 8


def draw_hidden_in(key, part):
    first_key, second_key, third_key = jax.random.split(key, 3)
    row_scale = jnp.exp(jax.random.uniform(first_key, (SEQS, SEQ_LEN, 1), jnp.float32, -1.15, 1.15))
    column_scale = jnp.exp(jax.random.uniform(second_key, (1, 1, D), jnp.float32, -1.15, 1.15))
    base_value = jnp.clip(jax.random.normal(third_key, (SEQS, SEQ_LEN, D), jnp.float32), -4.0, 4.0)
    return (base_value * row_scale * column_scale).astype(jnp.bfloat16)


def draw_segment_ids(key, part):
    first_key, second_key, third_key = jax.random.split(key, 3)
    rates = jax.random.randint(first_key, (SEQS, 1), 0, 3)
    period = jnp.where(rates == 0, 2, jnp.where(rates == 1, 8, 64)).astype(jnp.int32)
    ticks = jax.random.randint(second_key, (SEQS, SEQ_LEN), 0, 1 << 20)
    places = jnp.arange(SEQ_LEN, dtype=jnp.int32)[None, :]
    aligned = places % 8 == 0
    starts = (ticks % period == 0) & aligned
    chosen_one = jax.random.randint(third_key, (SEQS // SEQ_B,), 0, SEQ_B)
    row_index = jnp.arange(SEQS, dtype=jnp.int32)
    single_doc = row_index % SEQ_B == chosen_one[row_index // SEQ_B]
    dense_row = row_index == (chosen_one[0] + 1) % SEQ_B
    starts = jnp.where(dense_row[:, None], aligned, starts)
    starts = starts & (places > 0)
    starts = starts & jnp.logical_not(single_doc)[:, None]
    return jnp.cumsum(starts.astype(jnp.int32), axis=1).astype(jnp.int32)


def spiked(values, rng, source, target, shards_of, factor):
    def block_of(dim):
        return (jnp.arange(values.shape[dim]) // (values.shape[dim] // shards_of)).reshape((-1,) + (1,) * (values.ndim - 1 - dim))

    near = jax.random.permutation(rng, shards_of)[block_of(target)]
    second = (block_of(target) + shards_of // 2) % shards_of
    return jnp.where((block_of(source) == near) | (block_of(source) == second), factor * values, values)


def block_levels(key, shape, shards, least, top_value):
    factor_of, own = 1.0, jax.random.fold_in(key, 6)
    for axis_at, blocks in shards:
        draws = jnp.exp(jax.random.uniform(jax.random.fold_in(own, axis_at), (blocks,), jnp.float32, least / len(shards), top_value / len(shards)))
        factor_of = factor_of * jnp.repeat(draws, shape[axis_at] // blocks).reshape([-1 if axis == axis_at else 1 for axis in range(len(shape))])
    return factor_of


def normal_values(stream_key, shape, deviation, bound, cuts=(), kind=jnp.bfloat16):
    factor_of = block_levels(stream_key, shape, cuts, -0.22, 0.18) if cuts else 1.0
    values = jax.random.normal(stream_key, shape, jnp.float32) * deviation * factor_of
    return jnp.minimum(jnp.maximum(values, -bound), bound).astype(kind)


def bell_draw_with(rng, extent, width, most, cuts, heavy, kind=jnp.bfloat16):
    array = width * jax.random.normal(rng, extent, jnp.float32)
    if cuts:
        array = array * block_levels(rng, extent, cuts, -0.22, 0.18)
    return jnp.clip(spiked(array, jax.random.fold_in(rng, 3), *heavy), -most, most).astype(kind)


def setup_inputs(seed: int = 0) -> dict:
    arg_keys = jax.random.split(jax.random.key(seed), 13)
    return {
        "hidden_in": draw_hidden_in(jax.random.fold_in(arg_keys[12], 71), 0),
        "attn_gain": jnp.clip(1.0 + 0.15 * jax.random.normal(arg_keys[1], (D,), jnp.float32), 0.25, 1.75).astype(jnp.bfloat16),
        "query_weight": normal_values(arg_keys[2], (D, HEADS * HEAD_DIM), D ** -0.5, 0.125, ((0, 32),)),
        "key_weight": normal_values(arg_keys[3], (D, KV_HEADS * HEAD_DIM), D ** -0.5, 0.125, ((0, 32),)),
        "value_weight": normal_values(arg_keys[4], (D, KV_HEADS * HEAD_DIM), D ** -0.5, 0.125, ((0, 32),)),
        "out_weight": normal_values(arg_keys[5], (D, HEADS * HEAD_DIM), (max(HEADS * HEAD_DIM // 32, 1)) ** -0.5, 0.625, ((0, 32),)),
        "mlp_gain": jnp.clip(1.0 + 0.15 * jax.random.normal(arg_keys[6], (D,), jnp.float32), 0.25, 1.75).astype(jnp.bfloat16),
        "gate_weight": normal_values(arg_keys[7], (D, FF), D ** -0.5, 0.125, ((0, 32),)),
        "up_weight": normal_values(arg_keys[8], (D, FF), D ** -0.5, 0.125, ((0, 32),)),
        "down_weight": normal_values(arg_keys[9], (D, FF), FF ** -0.5, 0.078125, ((0, 32),)),
        "segment_ids": draw_segment_ids(jax.random.fold_in(arg_keys[12], 71), 0),
        "grad_output": bell_draw_with(arg_keys[11], (SEQS, SEQ_LEN, D), 1.0, 6.0, ((0, 4), (1, 8)), (1, 2, 8, 2.0)),
    }


EPSILON = 1e-05
ROPE_BASE = 10000.0
HIGHEST_PRECISION = lax.Precision.HIGHEST

@jax.custom_vjp
def low(v):
    return lax.optimization_barrier(v.astype(jnp.bfloat16)).astype(jnp.float32)

@jax.custom_vjp
def low_back(v):
    return v

def low_keep(v):
    return (low(v), None)

def low_pass(kept, grad):
    return (grad,)

def back_keep(v):
    return (v, None)

def back_low(kept, grad):
    return (low(grad),)
low.defvjp(low_keep, low_pass)
low_back.defvjp(back_keep, back_low)

def rotate(values, cosine, sine_table):
    half_dim = values.shape[-1] // 2
    first_half = values[..., :half_dim]
    second_half = values[..., half_dim:]
    return jnp.concatenate([first_half * cosine - second_half * sine_table, second_half * cosine + first_half * sine_table], -1)

def norm_rows(values):
    return values * lax.rsqrt(lax.optimization_barrier(jnp.mean(values * values, -1, keepdims=True)) + EPSILON)

def attend_one(entries):
    query_seq, key_seq, value_seq, segment = entries
    length = query_seq.shape[0]
    repeat = HEADS // KV_HEADS
    scaling = 1.0 / math.sqrt(HEAD_DIM)
    grouped = query_seq.reshape(length, KV_HEADS, repeat, HEAD_DIM)
    scores = low_back(jnp.einsum('igrd,jgd->grij', grouped, key_seq, precision=HIGHEST_PRECISION) * scaling)
    positions = jnp.arange(length, dtype=jnp.int32)
    allowed = (segment[:, None] == segment[None, :]) & (positions[None, :] <= positions[:, None])
    scores = jnp.where(allowed, scores, -1e+30)
    highest = lax.optimization_barrier(jnp.max(scores, -1, keepdims=True))
    weight = jnp.exp(scores - highest)
    probabilities = weight / lax.optimization_barrier(jnp.sum(weight, -1, keepdims=True))
    mixed_heads = jnp.einsum('grij,jgd->igrd', low(probabilities), value_seq, precision=HIGHEST_PRECISION)
    return mixed_heads.reshape(length, HEADS * HEAD_DIM)

def block_forward(source_block, segments, params, cosine, sine_table):
    attn_gain, query_weight, key_weight, value_weight, out_weight, mlp_gain, gate_weight, up_weight, down_weight = params
    number = source_block.shape[0]
    normed = low(norm_rows(source_block) * attn_gain)
    queries = low_back(jnp.einsum('bld,de->ble', normed, query_weight, precision=HIGHEST_PRECISION))
    key_rows = low_back(jnp.einsum('bld,de->ble', normed, key_weight, precision=HIGHEST_PRECISION))
    value_rows = low(low_back(jnp.einsum('bld,de->ble', normed, value_weight, precision=HIGHEST_PRECISION)))
    queries = low(rotate(queries.reshape(number, SEQ_LEN, HEADS, HEAD_DIM), cosine, sine_table))
    key_rows = low(rotate(key_rows.reshape(number, SEQ_LEN, KV_HEADS, HEAD_DIM), cosine, sine_table))
    value_rows = value_rows.reshape(number, SEQ_LEN, KV_HEADS, HEAD_DIM)
    mixed_heads = lax.map(jax.checkpoint(attend_one), (queries, key_rows, value_rows, segments))
    mixed_heads = low(low_back(mixed_heads))
    middle = source_block + low_back(jnp.einsum('ble,de->bld', mixed_heads, out_weight, precision=HIGHEST_PRECISION))
    normed_two = low(norm_rows(middle) * mlp_gain)
    gate_value = low_back(jnp.einsum('bld,df->blf', normed_two, gate_weight, precision=HIGHEST_PRECISION))
    up_value = low_back(jnp.einsum('bld,df->blf', normed_two, up_weight, precision=HIGHEST_PRECISION))
    active = low(jax.nn.silu(gate_value) * up_value)
    return middle + low_back(jnp.einsum('blf,df->bld', active, down_weight, precision=HIGHEST_PRECISION))

def reference(hidden_in, attn_gain, query_weight, key_weight, value_weight, out_weight, mlp_gain, gate_weight, up_weight, down_weight, segment_ids, grad_output):
    weights = tuple((matrix.astype(jnp.float32) for matrix in (attn_gain, query_weight, key_weight, value_weight, out_weight, mlp_gain, gate_weight, up_weight, down_weight)))
    half_dim = HEAD_DIM // 2
    frequency = ROPE_BASE ** (-(jnp.arange(half_dim, dtype=jnp.float32) * 2.0 / HEAD_DIM))
    angles = jnp.arange(SEQ_LEN, dtype=jnp.float32)[:, None] * frequency[None, :]
    cosine = jnp.cos(angles)[:, None, :]
    sine_table = jnp.sin(angles)[:, None, :]
    group_size = math.gcd(SEQS, max(1, 4096 // SEQ_LEN))
    blocks = SEQS // group_size
    segments = segment_ids.reshape(blocks, group_size, SEQ_LEN)

    def forward(source, *params):
        shaped = source.reshape(blocks, group_size, SEQ_LEN, D)

        def step_block(state_carry, entries):
            return (state_carry, block_forward(entries[0], entries[1], params, cosine, sine_table))
        unused, outputs = lax.scan(step_block, jnp.zeros((), jnp.float32), (shaped, segments))
        return outputs.reshape(SEQS, SEQ_LEN, D)
    result, pullback = jax.vjp(forward, hidden_in.astype(jnp.float32), *weights)
    gradients = pullback(grad_output.astype(jnp.float32))
    return (result.astype(jnp.bfloat16), gradients[0], gradients[1], gradients[2], gradients[3], gradients[4], gradients[5], gradients[6], gradients[7], gradients[8], gradients[9])
```

```python
import math

import jax
import jax.numpy as jnp
from jax import lax
from jax.sharding import Mesh
from jax.sharding import PartitionSpec as P

HEADS = 32
KV_HEADS = 8
HEAD_DIM = 80
HALF = HEAD_DIM // 2
REPEAT = HEADS // KV_HEADS

EPSILON = 1e-05
ROPE_BASE = 10000.0

CHIPS = 4
SPLIT = 2 * CHIPS
PLANE = ("y", "core", "lo")
EVERY = ("y", "core", "hi", "lo")


def dot(left, right):
    return lax.dot_general(
        left, right, (((1,), (0,)), ((), ())), preferred_element_type=jnp.float32
    )


def by_columns(left, right):
    return lax.dot_general(
        left, right, (((1,), (1,)), ((), ())), preferred_element_type=jnp.float32
    )


def by_rows(left, right):
    return lax.dot_general(
        left, right, (((0,), (0,)), ((), ())), preferred_element_type=jnp.float32
    )


def swap_core(value):
    return lax.ppermute(value, "core", [(0, 1), (1, 0)])


def swap_chip(value, step):
    return lax.ppermute(value, ("y", "lo"), [(chip, chip ^ step) for chip in range(CHIPS)])


def gather_plane(value):
    slots = []
    for step in range(CHIPS):
        here = value if step == 0 else swap_chip(value, step)
        slots += [here, swap_core(here)]
    return jnp.concatenate(slots, 0)


def scatter_plane(partial):
    rows, cols = partial.shape[0] // SPLIT, partial.shape[1]
    slots = partial.astype(jnp.bfloat16).reshape(CHIPS, 2, rows, cols)
    total = None
    for step in range(CHIPS - 1, -1, -1):
        pair = slots[step, 0].astype(jnp.float32) + swap_core(slots[step, 1]).astype(jnp.float32)
        if step:
            pair = swap_chip(pair.astype(jnp.bfloat16), step).astype(jnp.float32)
        total = pair if total is None else total + pair
    return total


def to_plane(weight):
    rows, cols = weight.shape[0], weight.shape[1] // SPLIT
    split = jnp.swapaxes(weight.reshape(rows, SPLIT, cols), 0, 1)
    return lax.all_to_all(split, PLANE, 0, 0, tiled=True).reshape(SPLIT * rows, cols)


def from_plane(grads):
    rows, cols = grads.shape[0] // SPLIT, grads.shape[1]
    back = lax.all_to_all(grads.reshape(SPLIT, rows, cols), PLANE, 0, 0, tiled=True)
    return jnp.swapaxes(back, 0, 1)


def along(weight):
    return lax.all_gather(weight, "hi", axis=0, tiled=True)


def sum_along(grads):
    return lax.psum_scatter(grads, "hi", scatter_dimension=0, tiled=True)


def by_step(value, at, axis):
    steps = [
        lax.dynamic_index_in_dim(value, at ^ step, axis) for step in range(value.shape[axis])
    ]
    return jnp.concatenate(steps, axis)


def rotate(values, cosine, sine_table):
    first_half, second_half = values[..., :HALF], values[..., HALF:]
    return jnp.concatenate(
        [
            first_half * cosine - second_half * sine_table,
            second_half * cosine + first_half * sine_table,
        ],
        -1,
    )


def shards(
    sizes,
    hidden_in,
    attn_gain,
    query_weight,
    key_weight,
    value_weight,
    out_weight,
    mlp_gain,
    gate_weight,
    up_weight,
    down_weight,
    segment_ids,
    grad_output,
):
    y_n, hi_n, lo_n = sizes
    batch_n = 2 * y_n
    seq_b, local_len, width = hidden_in.shape
    seq_len = segment_ids.shape[1]
    rows = seq_b * local_len
    tokens = SPLIT * rows
    own_rows = query_weight.shape[0]
    ff_width = gate_weight.shape[1]
    ff_pad = -(-ff_width // (SPLIT * 128)) * SPLIT * 128
    query_cols = HEADS * HEAD_DIM // SPLIT
    qkv_cols = query_cols + 2 * HEAD_DIM
    scaling = 1.0 / math.sqrt(HEAD_DIM)
    y_at, core_at = lax.axis_index("y"), lax.axis_index("core")
    hi_at, lo_at = lax.axis_index("hi"), lax.axis_index("lo")

    def reorder(value):
        lead = value.shape[:-1]
        value = value.reshape(lead + (batch_n, hi_n, lo_n * own_rows))
        return jnp.swapaxes(value, -3, -2).reshape(lead + (width,))

    def restore(value):
        lead = value.shape[:-1]
        value = value.reshape(lead + (hi_n, batch_n, lo_n * own_rows))
        return jnp.swapaxes(value, -3, -2).reshape(lead + (width,))

    offset = (hi_at * lo_n + lo_at) * local_len
    own_segments = lax.dynamic_slice_in_dim(segment_ids, offset, local_len, 1)
    small = jnp.concatenate(
        [attn_gain, mlp_gain, own_segments.astype(jnp.bfloat16).reshape(rows)]
    )
    small_pad = -(-small.shape[0] // 128) * 128
    small = jnp.pad(small, (0, small_pad - small.shape[0])).reshape(1, small_pad)
    small = lax.all_gather(small, EVERY, axis=0, tiled=True).astype(jnp.float32)
    small = small.reshape(batch_n, hi_n, lo_n, small_pad)
    gain_one = reorder(small[..., :own_rows].reshape(width))
    gain_two = reorder(small[..., own_rows : 2 * own_rows].reshape(width))
    segments = small[..., 2 * own_rows : 2 * own_rows + rows].reshape(
        y_n, 2, hi_n, lo_n, seq_b, local_len
    )
    segments = by_step(segments, y_at, 0)
    segments = by_step(segments, core_at, 1)
    segments = by_step(segments, lo_at, 3)
    segments = segments.transpose(0, 1, 4, 2, 3, 5)
    seqs = y_n * 2 * seq_b
    key_segments = segments.reshape(seqs, seq_len)
    queries_len = lo_n * local_len
    query_segments = lax.dynamic_index_in_dim(segments, hi_at, 3, keepdims=False).reshape(
        seqs, queries_len
    )
    lo_place = lo_at ^ jnp.arange(lo_n)
    inner = (lo_place[:, None] * local_len + jnp.arange(local_len)[None, :]).reshape(queries_len)
    query_place = hi_at * queries_len + inner
    key_place = (jnp.arange(hi_n)[:, None] * queries_len + inner[None, :]).reshape(seq_len)
    frequency = ROPE_BASE ** (-(jnp.arange(HALF, dtype=jnp.float32) * 2.0 / HEAD_DIM))
    angles = query_place.astype(jnp.float32)[:, None] * frequency[None, :]

    def table(values):
        values = values.reshape(1, lo_n, 1, 1, local_len, 1, HALF)
        values = jnp.broadcast_to(values, (y_n, lo_n, 2, seq_b, local_len, 1, HALF))
        return values.reshape(tokens, 1, HALF)

    cosine, sine_table = table(jnp.cos(angles)), table(jnp.sin(angles))

    heads_weight = jnp.concatenate(
        [
            query_weight.reshape(own_rows, SPLIT, query_cols),
            key_weight.reshape(own_rows, SPLIT, HEAD_DIM),
            value_weight.reshape(own_rows, SPLIT, HEAD_DIM),
            jnp.zeros((own_rows, SPLIT, 512 - qkv_cols), jnp.bfloat16),
            out_weight.reshape(own_rows, SPLIT, query_cols),
            jnp.zeros((own_rows, SPLIT, 384 - query_cols), jnp.bfloat16),
        ],
        -1,
    ).reshape(own_rows, SPLIT * 896)
    heads_plane = to_plane(heads_weight)
    qkv_full = along(heads_plane[:, :512])
    out_full = along(heads_plane[:, 512:])

    def widen(weight):
        return jnp.pad(weight, ((0, 0), (0, ff_pad - ff_width)))

    gate_full = along(to_plane(widen(gate_weight)))
    up_full = along(to_plane(widen(up_weight)))
    down_full = along(to_plane(widen(down_weight)))

    source = reorder(hidden_in.reshape(rows, width)).astype(jnp.float32)
    inv_one = lax.rsqrt(jnp.mean(source * source, -1, keepdims=True) + EPSILON)
    normed_one = source * inv_one
    normed_low = gather_plane((normed_one * gain_one).astype(jnp.bfloat16))
    cotangent = reorder(grad_output.reshape(rows, width))
    cotangent_all = gather_plane(cotangent)

    qkv = dot(normed_low, qkv_full)
    queries = rotate(qkv[:, :query_cols].reshape(tokens, REPEAT, HEAD_DIM), cosine, sine_table)
    key_rows = rotate(
        qkv[:, query_cols : query_cols + HEAD_DIM].reshape(tokens, 1, HEAD_DIM), cosine, sine_table
    )
    queries = queries.astype(jnp.bfloat16)
    key_value = jnp.concatenate(
        [key_rows.reshape(tokens, HEAD_DIM), qkv[:, query_cols + HEAD_DIM : qkv_cols]], 1
    ).astype(jnp.bfloat16)
    key_value = along(key_value)

    def by_seq(values):
        last = values.shape[1:]
        lead = values.shape[0] // tokens
        values = values.reshape((lead, y_n, lo_n, 2, seq_b, local_len) + last)
        values = values.transpose((1, 3, 4, 0, 2, 5) + tuple(range(6, 6 + len(last))))
        return values.reshape((seqs, lead * queries_len) + last)

    def by_token(values):
        last = values.shape[2:]
        lead = values.shape[1] // queries_len
        values = values.reshape((y_n, 2, seq_b, lead, lo_n, local_len) + last)
        values = values.transpose((3, 0, 4, 1, 2, 5) + tuple(range(6, 6 + len(last))))
        return values.reshape((lead * tokens,) + last)

    queries = by_seq(queries)
    key_value = by_seq(key_value)
    key_all, value_all = key_value[..., :HEAD_DIM], key_value[..., HEAD_DIM:]

    def scores_of(query_seq, key_seq, query_seg, key_seg):
        raw_scores = (
            jnp.einsum("ird,jd->rij", query_seq, key_seq, preferred_element_type=jnp.float32)
            * scaling
        )
        allowed = (query_seg[:, None] == key_seg[None, :]) & (
            key_place[None, :] <= query_place[:, None]
        )
        return jnp.where(allowed, raw_scores, -1e30)

    def attend(entries):
        query_seq, key_seq, value_seq, query_seg, key_seg = entries
        scores = scores_of(query_seq, key_seq, query_seg, key_seg)
        highest = jnp.max(scores, -1, keepdims=True)
        weight = jnp.exp(scores - highest)
        total = jnp.sum(weight, -1, keepdims=True)
        probabilities = (weight / total).astype(jnp.bfloat16)
        mixed_heads = jnp.einsum(
            "rij,jd->ird", probabilities, value_seq, preferred_element_type=jnp.float32
        )
        return mixed_heads.astype(jnp.bfloat16), highest + jnp.log(total)

    attended, log_total = lax.map(
        attend, (queries, key_all, value_all, query_segments, key_segments)
    )
    mixed_rows = by_token(attended).reshape(tokens, query_cols)
    mixed_rows = jnp.pad(mixed_rows, ((0, 0), (0, 384 - query_cols)))
    middle = source + scatter_plane(by_columns(mixed_rows, out_full))

    inv_two = lax.rsqrt(jnp.mean(middle * middle, -1, keepdims=True) + EPSILON)
    normed_two = middle * inv_two
    normed_mid = gather_plane((normed_two * gain_two).astype(jnp.bfloat16))
    gate_value = dot(normed_mid, gate_full)
    up_value = dot(normed_mid, up_full)
    active = (jax.nn.silu(gate_value) * up_value).astype(jnp.bfloat16)
    result = restore((middle + scatter_plane(by_columns(active, down_full))).astype(jnp.bfloat16))
    grad_active = dot(cotangent_all, down_full)
    sigmoid_gate = jax.nn.sigmoid(gate_value)
    grad_gate = (
        grad_active * up_value * sigmoid_gate * (1.0 + gate_value * (1.0 - sigmoid_gate))
    ).astype(jnp.bfloat16)
    grad_up = (grad_active * jax.nn.silu(gate_value)).astype(jnp.bfloat16)
    grad_norm_mid = scatter_plane(by_columns(grad_gate, gate_full) + by_columns(grad_up, up_full))
    gain_two_term = jnp.sum(grad_norm_mid * normed_two, 0)
    scaled_two = grad_norm_mid * gain_two
    grad_middle = cotangent.astype(jnp.float32) + inv_two * (
        scaled_two - normed_two * jnp.mean(scaled_two * normed_two, -1, keepdims=True)
    )

    def finish(left, right):
        return from_plane(sum_along(by_rows(left, right).astype(jnp.bfloat16)))

    def finish_mlp(left, right):
        grads = finish(left, right).reshape(own_rows, ff_pad)
        return grads[:, :ff_width].astype(jnp.float32)

    gate_grads = finish_mlp(normed_mid, grad_gate)
    up_grads = finish_mlp(normed_mid, grad_up)
    down_grads = finish_mlp(cotangent_all, active)

    grad_branch = gather_plane(grad_middle.astype(jnp.bfloat16))
    grad_mixed = dot(grad_branch, out_full)[:, :query_cols].astype(jnp.bfloat16)
    grad_mixed = by_seq(grad_mixed.reshape(tokens, REPEAT, HEAD_DIM))
    out_grads = finish(grad_branch, mixed_rows)[..., :query_cols].reshape(own_rows, -1)

    def attend_back(entries):
        query_seq, key_seq, value_seq, query_seg, key_seg, log_seq, grad_seq = entries
        scores = scores_of(query_seq, key_seq, query_seg, key_seg)
        probabilities = jnp.exp(scores - log_seq)
        grad_probs = jnp.einsum(
            "ird,jd->rij", grad_seq, value_seq, preferred_element_type=jnp.float32
        )
        centre = jnp.sum(probabilities * grad_probs, -1, keepdims=True)
        grad_scores = (probabilities * (grad_probs - centre)).astype(jnp.bfloat16)
        grad_values = jnp.einsum(
            "rij,ird->jd",
            probabilities.astype(jnp.bfloat16),
            grad_seq,
            preferred_element_type=jnp.float32,
        )
        grad_keys = (
            jnp.einsum("rij,ird->jd", grad_scores, query_seq, preferred_element_type=jnp.float32)
            * scaling
        )
        grad_queries = (
            jnp.einsum("rij,jd->ird", grad_scores, key_seq, preferred_element_type=jnp.float32)
            * scaling
        )
        return grad_queries, jnp.concatenate([grad_keys, grad_values], 1).astype(jnp.bfloat16)

    grad_queries, grad_key_value = lax.map(
        attend_back,
        (queries, key_all, value_all, query_segments, key_segments, log_total, grad_mixed),
    )
    grad_key_value = sum_along(by_token(grad_key_value)).astype(jnp.float32)
    grad_queries = rotate(by_token(grad_queries), cosine, -sine_table)
    grad_keys = rotate(
        grad_key_value[:, :HEAD_DIM].reshape(tokens, 1, HEAD_DIM), cosine, -sine_table
    )
    grad_qkv = jnp.concatenate(
        [
            grad_queries.reshape(tokens, query_cols),
            grad_keys.reshape(tokens, HEAD_DIM),
            grad_key_value[:, HEAD_DIM:],
            jnp.zeros((tokens, 512 - qkv_cols), jnp.float32),
        ],
        1,
    ).astype(jnp.bfloat16)
    grad_norm_one = scatter_plane(by_columns(grad_qkv, qkv_full))
    gain_one_term = jnp.sum(grad_norm_one * normed_one, 0)
    scaled_one = grad_norm_one * gain_one
    grad_input = grad_middle + inv_one * (
        scaled_one - normed_one * jnp.mean(scaled_one * normed_one, -1, keepdims=True)
    )
    head_terms = jnp.concatenate(
        [
            by_rows(normed_low, grad_qkv)[:, :qkv_cols],
            gain_one_term[:, None],
            gain_two_term[:, None],
            jnp.zeros((width, 512 - qkv_cols - 2), jnp.float32),
        ],
        1,
    ).astype(jnp.bfloat16)
    head_grads = from_plane(sum_along(head_terms)).astype(jnp.float32)
    return (
        result.reshape(seq_b, local_len, width),
        restore(grad_input).reshape(seq_b, local_len, width),
        jnp.sum(head_grads[..., qkv_cols], 1),
        head_grads[..., :query_cols].reshape(own_rows, -1),
        head_grads[..., query_cols : query_cols + HEAD_DIM].reshape(own_rows, -1),
        head_grads[..., query_cols + HEAD_DIM : qkv_cols].reshape(own_rows, -1),
        out_grads.astype(jnp.float32),
        jnp.sum(head_grads[..., qkv_cols + 1], 1),
        gate_grads,
        up_grads,
        down_grads,
    )


def solution(mesh):
    batch_n, seq_n = mesh.shape["batch"], mesh.shape["seq"]
    y_n = batch_n // 2
    lo_n = CHIPS // y_n
    hi_n = seq_n // lo_n
    fine = Mesh(mesh.devices.reshape(y_n, 2, hi_n, lo_n), EVERY)
    token = P(("y", "core"), ("hi", "lo"), None)
    vector = P(EVERY)
    matrix = P(EVERY, None)
    in_specs = (
        token, vector, matrix, matrix, matrix, matrix, vector, matrix, matrix, matrix,
        P(("y", "core"), None), token,
    )
    out_specs = (
        token, token, vector, matrix, matrix, matrix, matrix, vector, matrix, matrix, matrix,
    )

    def run(*arrays):
        return shards((y_n, hi_n, lo_n), *arrays)

    return jax.shard_map(run, mesh=fine, in_specs=in_specs, out_specs=out_specs, check_vma=False)
```

```python
import functools
import math

import jax
import jax.numpy as jnp
from jax import lax
from jax.experimental import pallas as pl
from jax.experimental.pallas import tpu as pltpu
from jax.sharding import Mesh
from jax.sharding import PartitionSpec as P

HEADS = 32
KV_HEADS = 8
HEAD_DIM = 80
HALF = HEAD_DIM // 2
REPEAT = HEADS // KV_HEADS

EPSILON = 1e-05
ROPE_BASE = 10000.0

CHIPS = 4
SPLIT = 2 * CHIPS
GROUP = ("y", "core", "lo")
EVERY = ("y", "core", "hi", "lo")


def dot(left, right):
    return lax.dot_general(
        left, right, (((1,), (0,)), ((), ())), preferred_element_type=jnp.float32
    )


def by_columns(left, right):
    return lax.dot_general(
        left, right, (((1,), (1,)), ((), ())), preferred_element_type=jnp.float32
    )


def by_rows(left, right):
    return lax.dot_general(
        left, right, (((0,), (0,)), ((), ())), preferred_element_type=jnp.float32
    )


def swap(value, axis, step, size):
    return lax.ppermute(value, axis, [(place, place ^ step) for place in range(size)])


def to_group(weight):
    rows, cols = weight.shape[0], weight.shape[1] // SPLIT
    split = jnp.swapaxes(weight.reshape(rows, SPLIT, cols), 0, 1)
    return lax.all_to_all(split, GROUP, 0, 0, tiled=True).reshape(SPLIT * rows, cols)


def from_group(grads):
    rows, cols = grads.shape[0] // SPLIT, grads.shape[1]
    return lax.all_to_all(grads.reshape(SPLIT, rows, cols), GROUP, 0, 0, tiled=True)


def along(value):
    return lax.all_gather(value, "hi", axis=0, tiled=True)


def sum_along(value):
    return lax.psum_scatter(value, "hi", scatter_dimension=0, tiled=True)


MESH = pl.DeviceIdType.MESH
HALVES = 2


def places():
    chip = lax.axis_index("y") * lax.axis_size("lo") + lax.axis_index("lo")
    near = chip + 1 - 2 * lax.rem(chip, 2)
    return lax.axis_index("core"), (chip, near, lax.rem(chip + 2, CHIPS), CHIPS - 1 - chip)


def device_at(chip, core):
    lo_n = lax.axis_size("lo")
    return (lax.div(chip, lo_n), core, lax.axis_index("hi"), lax.rem(chip, lo_n))


def place_at(chip, core):
    lo_n = lax.axis_size("lo")
    return (lax.div(chip, lo_n) * 2 + core) * lo_n + lax.rem(chip, lo_n)


def peers():
    core, chips = places()
    return device_at(chips[0], 1 - core), device_at(chips[1], core), device_at(chips[2], core)


def along_hi(step):
    hi_n = lax.axis_size("hi")
    hi = lax.rem(lax.axis_index("hi") + step, hi_n)
    return lax.axis_index("y"), lax.axis_index("core"), hi, lax.axis_index("lo")


def exchange(source_of, dest_ref, sign, zero_ref, send_sem, recv_sem, fill_sem):
    hi_n, hi = lax.axis_size("hi"), lax.axis_index("hi")
    parts = []
    for step in range(1, hi_n):
        copy = pltpu.make_async_remote_copy(
            src_ref=source_of(step),
            dst_ref=dest_ref.at[step - 1],
            send_sem=send_sem.at[step - 1],
            recv_sem=recv_sem.at[step - 1],
            device_id=along_hi(step if sign > 0 else hi_n - step),
            device_id_type=MESH,
        )
        fill = pltpu.make_async_copy(zero_ref, dest_ref.at[step - 1], fill_sem.at[step - 1])
        down, up = hi >= step, hi + step < hi_n
        sends, gets = (up, down) if sign > 0 else (down, up)
        parts.append((copy, fill, sends, gets))

    def start():
        zero_ref[...] = jnp.zeros_like(zero_ref)
        for copy, fill, sends, gets in parts:
            pl.when(sends)(copy.start)
            pl.when(jnp.logical_not(gets))(fill.start)

    def wait():
        for copy, fill, sends, gets in parts:
            pl.when(sends)(copy.wait_send)
            pl.when(gets)(copy.wait_recv)
            pl.when(jnp.logical_not(gets))(fill.wait)

    return start, wait


def turn_scratch(shape, dtype, others):
    return [pltpu.VMEM(shape, dtype)] + [pltpu.SemaphoreType.DMA((others,))] * 3


def meet(devices):
    barrier = pltpu.get_barrier_semaphore()
    for device in devices:
        pl.semaphore_signal(barrier, inc=1, device_id=device, device_id_type=MESH)
    pl.semaphore_wait(barrier, len(devices))


def gather_dot_kernel(weights_n, gated, *refs):
    refs = list(refs)

    def take(count):
        taken = refs[:count]
        del refs[:count]
        return taken

    outs_n = 3 if gated else weights_n
    (x_ref,) = take(1)
    weight_refs = take(weights_n)
    (all_ref,) = take(1)
    out_refs = take(outs_n)
    (x_buf,) = take(1)
    weight_bufs = take(weights_n)
    out_bufs = take(outs_n)
    load_sem, weight_sem, keep_sem, out_sem, send_sem, recv_sem = refs
    core_peer, near_peer, far_peer = peers()
    rows = x_ref.shape[0]
    half = rows // HALVES

    def piece(ref, at):
        return ref.at[pl.ds(at * half, half)]

    def route(index, source, step, core, device):
        return [
            pltpu.make_async_remote_copy(
                src_ref=piece(source, at),
                dst_ref=piece(x_buf.at[step, core], at),
                send_sem=send_sem.at[index, at],
                recv_sem=recv_sem.at[index, at],
                device_id=device,
                device_id_type=MESH,
            )
            for at in range(HALVES)
        ]

    to_near = route(0, x_ref, 1, 0, near_peer)
    to_far = route(1, x_ref, 2, 0, far_peer)
    to_core = route(2, x_ref, 0, 1, core_peer)
    onward = route(3, x_buf.at[2, 0], 3, 0, near_peer)
    near_core = route(4, x_buf.at[1, 0], 1, 1, core_peer)
    far_core = route(5, x_buf.at[2, 0], 2, 1, core_peer)
    onward_core = route(6, x_buf.at[3, 0], 3, 1, core_peer)

    load = pltpu.make_async_copy(x_ref, x_buf.at[0, 0], load_sem)
    load.start()
    fetches = []
    for at in range(weights_n):
        fetch = pltpu.make_async_copy(weight_refs[at], weight_bufs[at], weight_sem.at[at])
        fetch.start()
        fetches.append(fetch)
    meet((core_peer, near_peer, far_peer))
    for at in range(HALVES):
        to_near[at].start()
        to_far[at].start()
    for at in range(HALVES):
        to_core[at].start()
    kept, stored = [], []

    def keep(step, core):
        copy = pltpu.make_async_copy(
            x_buf.at[step, core], all_ref.at[step, core], keep_sem.at[step, core]
        )
        copy.start()
        kept.append(copy)

    def compute(step, core):
        turn = len(stored) % 2
        if len(stored) >= 2:
            for copy in stored[-2]:
                copy.wait()
        values = [dot(x_buf[step, core], buf[...]) for buf in weight_bufs]
        if gated:
            gate, up = values
            values = [gate, up, gate / (1.0 + jnp.exp(-gate)) * up]
        copies = []
        for at, value in enumerate(values):
            out_bufs[at][turn] = value.astype(out_bufs[at].dtype)
            copy = pltpu.make_async_copy(
                out_bufs[at].at[turn], out_refs[at].at[step, core], out_sem.at[at, turn]
            )
            copy.start()
            copies.append(copy)
        stored.append(copies)

    load.wait()
    keep(0, 0)
    for fetch in fetches:
        fetch.wait()
    compute(0, 0)
    for at in range(HALVES):
        to_core[at].wait_recv()
    keep(0, 1)
    compute(0, 1)
    for at in range(HALVES):
        to_far[at].wait_recv()
        onward[at].start()
        far_core[at].start()
        to_near[at].wait_recv()
        near_core[at].start()
    keep(2, 0)
    keep(1, 0)
    compute(2, 0)
    compute(1, 0)
    for step, copies in ((2, far_core), (1, near_core)):
        for at in range(HALVES):
            copies[at].wait_recv()
        keep(step, 1)
        compute(step, 1)
    for at in range(HALVES):
        onward[at].wait_recv()
        onward_core[at].start()
    keep(3, 0)
    compute(3, 0)
    for at in range(HALVES):
        onward_core[at].wait_recv()
    keep(3, 1)
    compute(3, 1)
    for copies in (to_near, to_far, to_core, onward, near_core, far_core, onward_core):
        for copy in copies:
            copy.wait_send()
    for copy in kept:
        copy.wait()
    for copies in stored[-2:]:
        for copy in copies:
            copy.wait()


def gather_dot(value, weights, dtypes, collective_id, gated=False):
    rows, width = value.shape
    cols = [weight.shape[1] for weight in weights]
    out_cols = cols[:1] * 3 if gated else cols
    flops = 2 * SPLIT * rows * width * sum(cols)
    anywhere = pl.BlockSpec(memory_space=pl.ANY)
    return pl.pallas_call(
        functools.partial(gather_dot_kernel, len(weights), gated),
        in_specs=[anywhere] * (1 + len(weights)),
        out_specs=[anywhere] * (1 + len(out_cols)),
        out_shape=[jax.ShapeDtypeStruct((CHIPS, 2, rows, width), value.dtype)]
        + [
            jax.ShapeDtypeStruct((CHIPS, 2, rows, count), dtype)
            for count, dtype in zip(out_cols, dtypes)
        ],
        scratch_shapes=[pltpu.VMEM((CHIPS, 2, rows, width), value.dtype)]
        + [pltpu.VMEM((width, count), jnp.bfloat16) for count in cols]
        + [pltpu.VMEM((2, rows, count), dtype) for count, dtype in zip(out_cols, dtypes)]
        + [
            pltpu.SemaphoreType.DMA,
            pltpu.SemaphoreType.DMA((len(weights),)),
            pltpu.SemaphoreType.DMA((CHIPS, 2)),
            pltpu.SemaphoreType.DMA((len(out_cols), 2)),
            pltpu.SemaphoreType.DMA((7, HALVES)),
            pltpu.SemaphoreType.DMA((7, HALVES)),
        ],
        compiler_params=pltpu.CompilerParams(
            vmem_limit_bytes=60 << 20, collective_id=collective_id, has_side_effects=True
        ),
        cost_estimate=pl.CostEstimate(
            flops=flops * 6, bytes_accessed=SPLIT * rows * width * 4, transcendentals=0
        ),
        name=f"gather_dot_{collective_id}",
    )(value, *weights)


def dot_scatter_kernel(lefts_n, parts_n, extra, *refs):
    refs = list(refs)

    def take(count):
        taken = refs[:count]
        del refs[:count]
        return taken

    left_refs = take(lefts_n)
    weight_refs = take(lefts_n)
    extra_ref = take(extra)
    (out_ref,) = take(1)
    extra_out = take(extra)
    left_bufs = take(lefts_n)
    weight_bufs = take(lefts_n)
    core_out, core_in, chip_out, chip_in = take(4)
    left_sem, weight_sem, core_send, core_recv, chip_send, chip_recv = take(6)
    core_peer, near_peer, far_peer = peers()
    rows = left_refs[0].shape[2]
    cols = weight_refs[0].shape[0] // parts_n
    tile = 256 if cols % 256 == 0 else 128
    order = (3, 1, 2, 0)

    fetches = {}
    for part in range(parts_n):
        for at in range(lefts_n):
            fetches["weight", part, at] = pltpu.make_async_copy(
                weight_refs[at].at[pl.ds(part * cols, cols)],
                weight_bufs[at].at[pl.ds(part * cols, cols)],
                weight_sem.at[at, part],
            )
    for step in order:
        for core in (1, 0):
            for at in range(lefts_n):
                fetches[step, core, at] = pltpu.make_async_copy(
                    left_refs[at].at[step, core],
                    left_bufs[at].at[step, core],
                    left_sem.at[at, step, core],
                )
    for at in range(lefts_n):
        fetches["weight", 0, at].start()
    for step in order[:1]:
        for core in (1, 0):
            for at in range(lefts_n):
                fetches[step, core, at].start()
    for part in range(1, parts_n):
        for at in range(lefts_n):
            fetches["weight", part, at].start()
    for step in order[1:]:
        for core in (1, 0):
            for at in range(lefts_n):
                fetches[step, core, at].start()
    hi_n = lax.axis_size("hi")
    meet([core_peer, near_peer, far_peer] + [along_hi(step) for step in range(1, hi_n) if extra])
    if extra:
        start_turns, wait_turns = exchange(
            lambda step: extra_ref[0].at[step], extra_out[0], -1, *take(4)
        )
        start_turns()
    waited = set()

    def ready(*key):
        for at in range(lefts_n):
            if key + (at,) not in waited:
                waited.add(key + (at,))
                fetches[key + (at,)].wait()

    def product(step, core, part, place):
        total = None
        for left, weight in zip(left_bufs, weight_bufs):
            at = pl.multiple_of(part * cols + place * tile, tile)
            term = by_columns(left[step, core], weight[pl.ds(at, tile)])
            total = term if total is None else total + term
        return total

    def wide(part, place):
        return pl.ds(pl.multiple_of(part * cols + place * tile, tile), tile)

    def each_tile(body):
        def run(place, carry):
            body(place, pl.ds(pl.multiple_of(place * tile, tile), tile))
            return carry

        lax.fori_loop(0, cols // tile, run, 0)

    def core_copy(step, part):
        return pltpu.make_async_remote_copy(
            src_ref=core_out.at[step, part],
            dst_ref=core_in.at[step, part],
            send_sem=core_send.at[step, part],
            recv_sem=core_recv.at[step, part],
            device_id=core_peer,
            device_id_type=MESH,
        )

    def chip_copy(step, part):
        return pltpu.make_async_remote_copy(
            src_ref=chip_out.at[step - 1, part],
            dst_ref=chip_in.at[step - 1, part],
            send_sem=chip_send.at[step - 1, part],
            recv_sem=chip_recv.at[step - 1, part],
            device_id=far_peer if step == 2 else near_peer,
            device_id_type=MESH,
        )

    def other_core(step, part):
        ready("weight", part)
        ready(step, 1)

        def body(place, columns):
            core_out[step, part, :, columns] = product(step, 1, part, place).astype(jnp.bfloat16)

        each_tile(body)
        core_copy(step, part).start()

    def this_core(step, part):
        ready(step, 0)
        core_copy(step, part).wait_recv()
        if step == 2:
            chip_copy(3, part).wait_recv()

        def body(place, columns):
            total = product(step, 0, part, place)
            total += core_in[step, part, :, columns].astype(jnp.float32)
            if step == 2:
                total += chip_in[2, part, :, columns].astype(jnp.float32)
            if step:
                chip_out[step - 1, part, :, columns] = total.astype(jnp.bfloat16)
            else:
                out_ref[:, wide(part, place)] = total

        each_tile(body)
        if step:
            chip_copy(step, part).start()

    parts = range(parts_n)
    for step in (3, 1):
        for part in parts:
            other_core(step, part)
        for part in parts:
            this_core(step, part)
    for step in (2, 0):
        for part in parts:
            other_core(step, part)
    for part in parts:
        this_core(0, part)
    for part in parts:
        this_core(2, part)
    for step in (1, 2):
        for part in parts:
            chip_copy(step, part).wait_recv()
            columns = pl.ds(part * cols, cols)
            out_ref[:, columns] += chip_in[step - 1, part].astype(jnp.float32)
    for part in parts:
        for step in range(CHIPS):
            core_copy(step, part).wait_send()
            if step:
                chip_copy(step, part).wait_send()
    if extra:
        wait_turns()


def dot_scatter(lefts, weights, collective_id, extra=()):
    others = lax.axis_size("hi") - 1
    lefts = [left.reshape(CHIPS, 2, left.size // (SPLIT * left.shape[-1]), left.shape[-1]) for left in lefts]
    rows = lefts[0].shape[2]
    parts_n = 2
    cols = weights[0].shape[0] // parts_n
    depths = [left.shape[3] for left in lefts]
    flops = 2 * SPLIT * rows * cols * parts_n * sum(depths)
    anywhere = pl.BlockSpec(memory_space=pl.ANY)
    out, *received = pl.pallas_call(
        functools.partial(dot_scatter_kernel, len(lefts), parts_n, len(extra)),
        in_specs=[anywhere] * (2 * len(lefts) + len(extra)),
        out_specs=[pl.BlockSpec(memory_space=pltpu.VMEM)] + [anywhere] * len(extra),
        out_shape=[jax.ShapeDtypeStruct((rows, parts_n * cols), jnp.float32)]
        + [jax.ShapeDtypeStruct((others,) + array.shape[1:], array.dtype) for array in extra],
        scratch_shapes=[pltpu.VMEM((CHIPS, 2, rows, depth), jnp.bfloat16) for depth in depths]
        + [pltpu.VMEM((parts_n * cols, depth), jnp.bfloat16) for depth in depths]
        + [
            pltpu.VMEM((CHIPS, parts_n, rows, cols), jnp.bfloat16),
            pltpu.VMEM((CHIPS, parts_n, rows, cols), jnp.bfloat16),
            pltpu.VMEM((CHIPS - 1, parts_n, rows, cols), jnp.bfloat16),
            pltpu.VMEM((CHIPS - 1, parts_n, rows, cols), jnp.bfloat16),
            pltpu.SemaphoreType.DMA((len(lefts), CHIPS, 2)),
            pltpu.SemaphoreType.DMA((len(lefts), parts_n)),
            pltpu.SemaphoreType.DMA((CHIPS, parts_n)),
            pltpu.SemaphoreType.DMA((CHIPS, parts_n)),
            pltpu.SemaphoreType.DMA((CHIPS - 1, parts_n)),
            pltpu.SemaphoreType.DMA((CHIPS - 1, parts_n)),
        ]
        + [
            scratch
            for array in extra
            for scratch in turn_scratch(array.shape[1:], array.dtype, others)
        ],
        compiler_params=pltpu.CompilerParams(
            vmem_limit_bytes=60 << 20, collective_id=collective_id, has_side_effects=True
        ),
        cost_estimate=pl.CostEstimate(
            flops=flops * 6, bytes_accessed=SPLIT * rows * cols * parts_n * 4, transcendentals=0
        ),
        name=f"dot_scatter_{collective_id}",
    )(*lefts, *weights, *extra)
    return (out, *received) if extra else out


def shuffle_kernel(order, piece, x_ref, out_ref):
    rows = x_ref[...]
    out_ref[...] = jnp.concatenate([rows[:, at * piece : (at + 1) * piece] for at in order], 1)


def shuffle(value, order):
    rows, width = value.shape
    return pl.pallas_call(
        functools.partial(shuffle_kernel, order, width // len(order)),
        out_shape=jax.ShapeDtypeStruct(value.shape, value.dtype),
        compiler_params=params(),
        name="shuffle",
    )(value)


def products_kernel(lefts, *refs):
    left_refs, right_refs, out_ref = refs[: max(lefts) + 1], refs[max(lefts) + 1 : -1], refs[-1]
    at = 0
    for left, right_ref in zip(lefts, right_refs):
        cols = right_ref.shape[1]
        out_ref[:, at : at + cols] = by_rows(left_refs[left][...], right_ref[...]).astype(
            jnp.bfloat16
        )
        at += cols


def products(lefts, rights, block=256):
    arrays, uses = lefts
    tokens, width = arrays[0].shape
    total = sum(right.shape[1] for right in rights)
    return pl.pallas_call(
        functools.partial(products_kernel, uses),
        grid=(width // block,),
        in_specs=[pl.BlockSpec((tokens, block), lambda at: (0, at)) for _ in arrays]
        + [
            pl.BlockSpec((tokens, right.shape[1]), lambda at: (0, 0), pipeline_mode=pl.Buffered(1))
            for right in rights
        ],
        out_specs=pl.BlockSpec((block, total), lambda at: (at, 0)),
        out_shape=jax.ShapeDtypeStruct((width, total), jnp.bfloat16),
        compiler_params=params(),
        cost_estimate=pl.CostEstimate(
            flops=4 * tokens * width * total, bytes_accessed=2 * tokens * width, transcendentals=0
        ),
        name="products",
    )(*arrays, *rights)


def project_kernel(
    x_ref, weight_ref, cosine_ref, sine_ref, query_ref, key_value_ref
):
    rows = dot(x_ref[...], weight_ref[...])
    count = rows.shape[0] // cosine_ref.shape[1]
    cosine = jnp.concatenate([cosine_ref[0]] * count, 0)
    sine_table = jnp.concatenate([sine_ref[0]] * count, 0)
    turned = []
    for values in heads_of(rows, REPEAT + 1):
        first_half, second_half = values[:, :HALF], values[:, HALF:]
        turned += [
            first_half * cosine - second_half * sine_table,
            second_half * cosine + first_half * sine_table,
        ]
    query_ref[...] = jnp.concatenate(turned[: 2 * REPEAT], 1).astype(jnp.bfloat16)
    value = rows[:, HEAD_DIM * (REPEAT + 1) : HEAD_DIM * (REPEAT + 2)]
    both = jnp.concatenate(turned[2 * REPEAT :] + [value], 1).astype(jnp.bfloat16)
    length = cosine_ref.shape[1]
    key_value_ref[...] = jnp.concatenate(
        [both[length * at : length * (at + 1)] for at in range(count)], 1
    )


def spread_kernel(weights_n, extra, *refs):
    refs = list(refs)

    def take(count):
        taken = refs[:count]
        del refs[:count]
        return taken

    (x_ref,), weight_refs, extra_ref = take(1), take(weights_n), take(extra)
    (all_ref,), group_refs, extra_out = take(1), take(weights_n), take(extra)
    local_sem, send_sem, recv_sem, spread_send, spread_recv = take(5)
    core_peer, near_peer, far_peer = peers()
    core, chips = places()
    cols = group_refs[0].shape[2]
    own_place = place_at(chips[0], core)

    def route(index, source, step, to_core, device):
        return pltpu.make_async_remote_copy(
            src_ref=source,
            dst_ref=all_ref.at[step, to_core],
            send_sem=send_sem.at[index],
            recv_sem=recv_sem.at[index],
            device_id=device,
            device_id_type=MESH,
        )

    to_near = route(0, x_ref, 1, 0, near_peer)
    to_far = route(1, x_ref, 2, 0, far_peer)
    to_core = route(2, x_ref, 0, 1, core_peer)
    onward = route(3, all_ref.at[2, 0], 3, 0, near_peer)
    near_core = route(4, all_ref.at[1, 0], 1, 1, core_peer)
    far_core = route(5, all_ref.at[2, 0], 2, 1, core_peer)
    onward_core = route(6, all_ref.at[3, 0], 3, 1, core_peer)
    own = pltpu.make_async_copy(x_ref, all_ref.at[0, 0], local_sem.at[weights_n])
    own.start()
    mine = []
    for at in range(weights_n):
        columns = pl.ds(pl.multiple_of(own_place * cols, 128), cols)
        copy = pltpu.make_async_copy(
            weight_refs[at].at[:, columns], group_refs[at].at[own_place], local_sem.at[at]
        )
        copy.start()
        mine.append(copy)
    others = [(step, flip) for step in range(CHIPS) for flip in range(2)][1:]
    devices = [device_at(chips[step], 1 - core if flip else core) for step, flip in others]
    hi_n = lax.axis_size("hi")
    meet(devices + [along_hi(step) for step in range(1, hi_n) if extra])
    if extra:
        start_turns, wait_turns = exchange(lambda step: extra_ref[0], extra_out[0], 1, *take(4))
        start_turns()
    to_near.start()
    to_far.start()
    to_core.start()
    copies = []
    for at in range(weights_n):
        for index, (step, flip) in enumerate(others):
            place = place_at(chips[step], 1 - core if flip else core)
            columns = pl.ds(pl.multiple_of(place * cols, 128), cols)
            copies.append(
                pltpu.make_async_remote_copy(
                    src_ref=weight_refs[at].at[:, columns],
                    dst_ref=group_refs[at].at[own_place],
                    send_sem=spread_send.at[at, index],
                    recv_sem=spread_recv.at[at, index],
                    device_id=devices[index],
                    device_id_type=MESH,
                )
            )
    to_far.wait_recv()
    onward.start()
    far_core.start()
    to_near.wait_recv()
    near_core.start()
    for copy in copies:
        copy.start()
    onward.wait_recv()
    onward_core.start()
    for copy in (near_core, far_core, to_core, onward_core):
        copy.wait_recv()
    for copy in (to_near, to_far, to_core, onward, near_core, far_core, onward_core):
        copy.wait_send()
    for copy in copies:
        copy.wait()
    if extra:
        wait_turns()
    for copy in mine:
        copy.wait()
    own.wait()


def spread_and_gather(value, weights, collective_id, extra=()):
    others = lax.axis_size("hi") - 1
    rows, width = value.shape
    own_rows, cols = weights[0].shape[0], weights[0].shape[1] // SPLIT
    anywhere = pl.BlockSpec(memory_space=pl.ANY)
    count = len(weights)
    gathered, *groups = pl.pallas_call(
        functools.partial(spread_kernel, count, len(extra)),
        in_specs=[anywhere] * (1 + count + len(extra)),
        out_specs=[anywhere] * (1 + count + len(extra)),
        out_shape=[jax.ShapeDtypeStruct((CHIPS, 2, rows, width), value.dtype)]
        + [jax.ShapeDtypeStruct((SPLIT, own_rows, cols), jnp.bfloat16)] * count
        + [jax.ShapeDtypeStruct((others,) + array.shape, array.dtype) for array in extra],
        scratch_shapes=[
            pltpu.SemaphoreType.DMA((count + 1,)),
            pltpu.SemaphoreType.DMA((7,)),
            pltpu.SemaphoreType.DMA((7,)),
            pltpu.SemaphoreType.DMA((count, SPLIT - 1)),
            pltpu.SemaphoreType.DMA((count, SPLIT - 1)),
        ]
        + [scratch for array in extra for scratch in turn_scratch(array.shape, array.dtype, others)],
        compiler_params=pltpu.CompilerParams(
            vmem_limit_bytes=60 << 20, collective_id=collective_id, has_side_effects=True
        ),
        cost_estimate=pl.CostEstimate(
            flops=10**11, bytes_accessed=SPLIT * rows * width * 4, transcendentals=0
        ),
        name=f"spread_{collective_id}",
    )(value, *weights, *extra)
    groups[:count] = [group.reshape(SPLIT * own_rows, cols) for group in groups[:count]]
    return gathered, *groups


def after(value, *others):
    return lax.optimization_barrier((value,) + others)[0]


def by_step(value, at, axis):
    steps = [
        lax.dynamic_index_in_dim(value, at ^ step, axis) for step in range(value.shape[axis])
    ]
    return jnp.concatenate(steps, axis)


def params(limit=60):
    return pltpu.CompilerParams(vmem_limit_bytes=limit << 20)


def heads_of(values, count):
    return [values[:, HEAD_DIM * at : HEAD_DIM * (at + 1)] for at in range(count)]


def allow(key_seg_ref, key_place_ref, query_seg_ref, query_place_ref):
    allowed = (key_seg_ref[0] == query_seg_ref[0]) & (key_place_ref[...] <= query_place_ref[...])
    return jnp.where(allowed, 0.0, -1e30)


def unpack(own_ref, others_ref, pair_ref):
    pair, length = 2 * HEAD_DIM, own_ref.shape[0]
    count = own_ref.shape[1] // pair
    for case in range(count):

        @pl.when(pl.program_id(0) % count == case)
        def _():
            columns = slice(pair * case, pair * (case + 1))
            pair_ref[:length] = own_ref[:, columns]
            for step in range(others_ref.shape[0]):
                pair_ref[length * (step + 1) : length * (step + 2)] = others_ref[step, :, columns]


def attend_kernel(
    query_ref, own_ref, others_ref, key_seg_ref, key_place_ref, query_seg_ref, query_place_ref,
    mixed_ref, log_ref, bias_ref, pair_ref,
):
    queries_len = query_seg_ref.shape[2]
    seq_len = key_seg_ref.shape[1]
    to_log2 = 1.0 / math.sqrt(HEAD_DIM) / math.log(2.0)
    bias_ref[...] = allow(key_seg_ref, key_place_ref, query_seg_ref, query_place_ref)
    rows = query_ref[0, :, 0, 0].reshape(queries_len, REPEAT * HEAD_DIM)
    unpack(own_ref, others_ref, pair_ref)
    key_rows, value_rows = heads_of(pair_ref[...], 2)
    mixed = []
    for at, query_rows in enumerate(heads_of(rows, REPEAT)):
        scores = by_columns(key_rows, query_rows) * to_log2 + bias_ref[...]
        highest = jnp.max(scores, 0, keepdims=True)
        weight = jnp.exp2(scores - highest)
        total = jnp.sum(weight, 0, keepdims=True)
        probabilities = (weight * (1.0 / total)).astype(jnp.bfloat16)
        mixed.append(by_rows(value_rows, probabilities).T)
        log_ref[0, at : at + 1] = highest + jnp.log2(total)
    mixed.append(jnp.zeros((queries_len, mixed_ref.shape[5] - REPEAT * HEAD_DIM), jnp.float32))
    mixed = jnp.concatenate(mixed, 1).astype(jnp.bfloat16)
    mixed_ref[0, :, 0, 0] = mixed.reshape(mixed_ref.shape[1], mixed_ref.shape[4], mixed.shape[1])


def attend_back_kernel(
    query_ref, own_ref, others_ref, grad_ref, log_ref, key_seg_ref, key_place_ref, query_seg_ref,
    query_place_ref, cosine_ref, sine_ref, grad_query_ref, grad_key_value_ref, bias_ref, pair_ref,
):
    queries_len = query_seg_ref.shape[2]
    seq_len = key_seg_ref.shape[1]
    scaling = 1.0 / math.sqrt(HEAD_DIM)
    to_log2 = scaling / math.log(2.0)
    bias_ref[...] = allow(key_seg_ref, key_place_ref, query_seg_ref, query_place_ref)
    query_rows = query_ref[0, :, 0, 0].reshape(queries_len, REPEAT * HEAD_DIM)
    grad_rows = grad_ref[0, :, 0, 0].reshape(queries_len, grad_ref.shape[5])
    unpack(own_ref, others_ref, pair_ref)
    key_rows, value_rows = heads_of(pair_ref[...], 2)
    cosine, sine_table = cosine_ref[...], sine_ref[...]
    grad_keys = jnp.zeros((seq_len, HEAD_DIM), jnp.float32)
    grad_values = jnp.zeros((seq_len, HEAD_DIM), jnp.float32)
    grad_queries = []
    for at in range(REPEAT):
        query, grad = heads_of(query_rows, REPEAT)[at], heads_of(grad_rows, REPEAT)[at]
        scores = by_columns(key_rows, query) * to_log2 + bias_ref[...]
        probabilities = jnp.exp2(scores - log_ref[0, at : at + 1])
        grad_probs = by_columns(value_rows, grad)
        centre = jnp.sum(probabilities * grad_probs, 0, keepdims=True)
        grad_scores = (probabilities * (grad_probs - centre)).astype(jnp.bfloat16)
        grad_values += dot(probabilities.astype(jnp.bfloat16), grad)
        grad_keys += dot(grad_scores, query)
        turned = by_rows(key_rows, grad_scores) * scaling
        first_half, second_half = turned[:HALF], turned[HALF:]
        turned = jnp.concatenate(
            [
                first_half * cosine + second_half * sine_table,
                second_half * cosine - first_half * sine_table,
            ],
            0,
        )
        grad_queries.append(turned.T)
    grad_queries = jnp.concatenate(grad_queries, 1).astype(jnp.bfloat16)
    grad_query_ref[0, :, 0, 0] = grad_queries.reshape(
        grad_query_ref.shape[1], grad_query_ref.shape[4], grad_queries.shape[1]
    )
    both = jnp.concatenate([grad_keys * scaling, grad_values], 1).astype(jnp.bfloat16)
    both = both.reshape(grad_key_value_ref.shape[0], queries_len, 2 * HEAD_DIM)
    count = grad_key_value_ref.shape[2] // (2 * HEAD_DIM)
    for case in range(count):

        @pl.when(pl.program_id(0) % count == case)
        def _():
            columns = slice(2 * HEAD_DIM * case, 2 * HEAD_DIM * (case + 1))
            grad_key_value_ref[:, :, columns] = both


def unrotate_kernel(grad_query_ref, own_ref, others_ref, cosine_ref, sine_ref, grad_ref):
    cosine, sine_table = cosine_ref[0], sine_ref[0]
    total = own_ref[0].astype(jnp.float32)
    for step in range(others_ref.shape[0]):
        total += others_ref[step].astype(jnp.float32)
    for at in range(grad_ref.shape[1] * grad_ref.shape[2]):
        place = (0, at // grad_ref.shape[2], at % grad_ref.shape[2])
        rows = total[:, 2 * HEAD_DIM * at : 2 * HEAD_DIM * (at + 1)]
        first_half, second_half = rows[:, :HALF], rows[:, HALF:HEAD_DIM]
        turned = jnp.concatenate(
            [
                first_half * cosine + second_half * sine_table,
                second_half * cosine - first_half * sine_table,
                rows[:, HEAD_DIM:],
                jnp.zeros((rows.shape[0], grad_ref.shape[4] - (REPEAT + 2) * HEAD_DIM), jnp.float32),
            ],
            1,
        ).astype(jnp.bfloat16)
        grad_ref[place] = jnp.concatenate([grad_query_ref[place], turned], 1)


def shards(
    sizes,
    hidden_in,
    attn_gain,
    query_weight,
    key_weight,
    value_weight,
    out_weight,
    mlp_gain,
    gate_weight,
    up_weight,
    down_weight,
    segment_ids,
    grad_output,
):
    y_n, hi_n, lo_n = sizes
    seq_b, local_len, width = hidden_in.shape
    seq_len = segment_ids.shape[1]
    rows = seq_b * local_len
    tokens = SPLIT * rows
    own_rows = query_weight.shape[0]
    ff_width = gate_weight.shape[1]
    ff_pad = -(-ff_width // (SPLIT * 128)) * SPLIT * 128
    query_cols = HEADS * HEAD_DIM // SPLIT
    qkv_cols = query_cols + 2 * HEAD_DIM
    y_at, core_at = lax.axis_index("y"), lax.axis_index("core")
    hi_at, lo_at = lax.axis_index("hi"), lax.axis_index("lo")

    pieces = [(outer, at) for at in range(hi_n) for outer in range(2 * y_n)]
    order = [outer * hi_n + at for outer, at in pieces]
    back = [order.index(at) for at in range(len(order))]

    offset = (hi_at * lo_n + lo_at) * local_len
    own_segments = lax.dynamic_slice_in_dim(segment_ids, offset, local_len, 1)
    small = jnp.concatenate(
        [attn_gain, mlp_gain, own_segments.astype(jnp.bfloat16).reshape(rows)]
    )
    small_pad = -(-small.shape[0] // 128) * 128
    small = jnp.pad(small, (0, small_pad - small.shape[0])).reshape(1, 1, 1, 1, small_pad)
    for axis, name, size in ((3, "lo", lo_n), (1, "core", 2), (0, "y", y_n), (2, "hi", hi_n)):
        steps = [small] + [swap(small, name, step, size) for step in range(1, size)]
        small = jnp.concatenate(steps, axis)
    small = small.astype(jnp.float32)

    def gain_of(values):
        for at, axis in ((y_at, 0), (core_at, 1), (hi_at, 2), (lo_at, 3)):
            values = by_step(values, at, axis)
        return values.transpose(2, 0, 1, 3, 4).reshape(width)

    gain_one = gain_of(small[..., :own_rows])
    gain_two = gain_of(small[..., own_rows : 2 * own_rows])
    segments = small[..., 2 * own_rows : 2 * own_rows + rows]
    segments = segments.reshape(y_n, 2, hi_n, lo_n, seq_b, local_len)
    segments = by_step(segments, hi_at, 2).transpose(0, 1, 4, 2, 3, 5)
    steps = [(hi_at - step) % hi_n for step in range(hi_n)]
    segments = jnp.concatenate(
        [lax.dynamic_index_in_dim(segments, step, 3) for step in steps], 3
    )
    seqs = y_n * 2 * seq_b
    queries_len = lo_n * local_len
    key_segments = segments.reshape(seqs, seq_len)
    query_segments = key_segments[:, :queries_len]
    lo_place = lo_at ^ jnp.arange(lo_n)
    inner = (lo_place[:, None] * local_len + jnp.arange(local_len)[None, :]).reshape(queries_len)
    query_place = hi_at * queries_len + inner
    key_place = (hi_at - jnp.arange(hi_n)) % hi_n
    key_place = (key_place[:, None] * queries_len + inner[None, :]).reshape(seq_len)
    place_shape = (lo_n, local_len)
    frequency = ROPE_BASE ** (-(jnp.arange(HALF, dtype=jnp.float32) * 2.0 / HEAD_DIM))
    angles = query_place.astype(jnp.float32)[:, None] * frequency[None, :]
    cosine, sine_table = jnp.cos(angles), jnp.sin(angles)

    def spread(*groups):
        pieces = []
        for group, total in zip(groups[::2], groups[1::2]):
            pieces += [piece.reshape(own_rows, SPLIT, -1) for piece in group]
            empty = total - sum(piece.size // (own_rows * SPLIT) for piece in group)
            if empty:
                pieces.append(jnp.zeros((own_rows, SPLIT, empty), jnp.bfloat16))
        return to_group(jnp.concatenate(pieces, -1).reshape(own_rows, -1))

    def widen(weight):
        return jnp.pad(weight, ((0, 0), (0, ff_pad - ff_width)))

    def everywhere(weight):
        return along(weight)

    first_group = spread(
        [query_weight, key_weight, value_weight], 512, [out_weight], 512, [widen(gate_weight)], ff_pad // SPLIT
    )
    qkv_full = everywhere(first_group[:, :512])
    out_full = everywhere(first_group[:, 512:1024])
    gate_full = everywhere(first_group[:, 1024:])

    source = shuffle(hidden_in.reshape(rows, width), order).astype(jnp.float32)
    inv_one = lax.rsqrt(jnp.mean(source * source, -1, keepdims=True) + EPSILON)
    normed_one = source * inv_one
    normed_low, up_group = spread_and_gather(
        (normed_one * gain_one).astype(jnp.bfloat16), [widen(up_weight)], 0
    )
    normed_low = normed_low.reshape(tokens, width)
    slots = (y_n, lo_n, 2, seq_b, local_len)
    packed = 2 * seq_b * 2 * HEAD_DIM

    def over_slots(cols):
        return pl.BlockSpec((1, 2, seq_b, local_len, cols), lambda lo: (lo, 0, 0, 0, 0))

    def slot_table():
        return pl.BlockSpec((1, local_len, HALF), lambda chip: (chip % lo_n, 0, 0))

    def slot_rows(cols):
        return pl.BlockSpec((2 * rows, cols), lambda lo: (lo, 0))

    queries, key_value = pl.pallas_call(
        project_kernel,
        grid=(CHIPS,),
        in_specs=[
            slot_rows(width),
            pl.BlockSpec((width, 512), lambda lo: (0, 0), pipeline_mode=pl.Buffered(1)),
            slot_table(),
            slot_table(),
        ],
        out_specs=[slot_rows(query_cols), pl.BlockSpec((local_len, packed), lambda lo: (lo, 0))],
        out_shape=[
            jax.ShapeDtypeStruct((tokens, query_cols), jnp.bfloat16),
            jax.ShapeDtypeStruct((CHIPS * local_len, packed), jnp.bfloat16),
        ],
        compiler_params=params(),
        name="project",
    )(
        normed_low,
        qkv_full,
        cosine.reshape(place_shape + (HALF,)),
        sine_table.reshape(place_shape + (HALF,)),
    )
    queries = queries.reshape(slots + (query_cols,))
    cotangent = shuffle(grad_output.reshape(rows, width), order)
    cotangent_all, down_group, others = spread_and_gather(
        cotangent, [widen(down_weight)], 7, (key_value,)
    )
    cotangent_all = cotangent_all.reshape(tokens, width)
    up_full = everywhere(up_group)
    down_full = everywhere(down_group)


    def of_seq(at):
        return at // (2 * seq_b), 0, at // seq_b % 2, at % seq_b, 0, 0

    def per_seq(cols):
        return pl.BlockSpec((1, lo_n, 1, 1, local_len, cols), of_seq)

    own_spec = pl.BlockSpec((queries_len, packed), lambda at: (at // (2 * seq_b), 0))
    others_spec = pl.BlockSpec(
        (hi_n - 1, queries_len, packed), lambda at: (0, at // (2 * seq_b), 0)
    )
    pair_scratch = pltpu.VMEM((seq_len, 2 * HEAD_DIM), jnp.bfloat16)
    log_spec = pl.BlockSpec((1, REPEAT, queries_len), lambda at: (at, 0, 0))
    mask_specs = [
        pl.BlockSpec((1, seq_len, 1), lambda at: (at, 0, 0)),
        pl.BlockSpec((seq_len, 1), lambda at: (0, 0)),
        pl.BlockSpec((1, 1, queries_len), lambda at: (at, 0, 0)),
        pl.BlockSpec((1, queries_len), lambda at: (0, 0)),
    ]
    masks = (
        key_segments.reshape(seqs, seq_len, 1),
        key_place.reshape(seq_len, 1),
        query_segments.reshape(seqs, 1, queries_len),
        query_place.reshape(1, queries_len),
    )
    mixed_rows, log_total = pl.pallas_call(
        attend_kernel,
        grid=(seqs,),
        in_specs=[per_seq(query_cols), own_spec, others_spec] + mask_specs,
        out_specs=[per_seq(512), log_spec],
        out_shape=[
            jax.ShapeDtypeStruct(slots + (512,), jnp.bfloat16),
            jax.ShapeDtypeStruct((seqs, REPEAT, queries_len), jnp.float32),
        ],
        scratch_shapes=[pltpu.VMEM((seq_len, queries_len), jnp.float32), pair_scratch],
        compiler_params=params(),
        name="attend",
    )(queries, key_value, others, *masks)
    mixed_rows = mixed_rows.reshape(tokens, 512)
    middle = source + dot_scatter([mixed_rows], [out_full], 1)

    inv_two = lax.rsqrt(jnp.mean(middle * middle, -1, keepdims=True) + EPSILON)
    normed_two = middle * inv_two
    normed_mid, gate_value, up_value, active = gather_dot(
        (normed_two * gain_two).astype(jnp.bfloat16),
        [gate_full, up_full],
        (jnp.float32, jnp.float32, jnp.bfloat16),
        2,
        gated=True,
    )
    normed_mid = normed_mid.reshape(tokens, width)
    gate_value = gate_value.reshape(tokens, -1)
    up_value = up_value.reshape(tokens, -1)
    active = active.reshape(tokens, -1)
    grad_active = dot(cotangent_all, down_full)
    sigmoid_gate = jax.nn.sigmoid(gate_value)
    grad_gate = (
        grad_active * up_value * sigmoid_gate * (1.0 + gate_value * (1.0 - sigmoid_gate))
    ).astype(jnp.bfloat16)
    grad_up = (grad_active * jax.nn.silu(gate_value)).astype(jnp.bfloat16)
    grad_norm_mid = dot_scatter([grad_gate, grad_up], [gate_full, up_full], 4)
    scaled_two = grad_norm_mid * gain_two
    grad_middle = cotangent.astype(jnp.float32) + inv_two * (
        scaled_two - normed_two * jnp.mean(scaled_two * normed_two, -1, keepdims=True)
    )

    def finish(back):
        return jnp.swapaxes(back, 0, 1).astype(jnp.float32)

    gate_up_product = products(([normed_mid], (0, 0)), [grad_gate, grad_up])
    gate_up_summed = sum_along(gate_up_product)
    gate_up_back = from_group(gate_up_summed)
    gate_up_grads = finish(gate_up_back)
    gate_grads = gate_up_grads[..., : ff_pad // SPLIT].reshape(own_rows, ff_pad)[:, :ff_width]
    up_grads = gate_up_grads[..., ff_pad // SPLIT :].reshape(own_rows, ff_pad)[:, :ff_width]
    grad_middle = after(grad_middle, gate_up_product)

    grad_branch, grad_mixed = gather_dot(
        grad_middle.astype(jnp.bfloat16), [out_full], (jnp.bfloat16,), 5
    )
    grad_branch = grad_branch.reshape(tokens, width)
    down_product = products(([after(cotangent_all, grad_mixed)], (0,)), [active])
    grad_mixed = after(grad_mixed, down_product)
    down_summed = sum_along(after(down_product, gate_up_summed))
    down_back = from_group(down_summed)
    down_grads = finish(down_back).reshape(own_rows, ff_pad)[:, :ff_width]

    grad_queries, grad_key_value = pl.pallas_call(
        attend_back_kernel,
        grid=(seqs,),
        in_specs=[per_seq(query_cols), own_spec, others_spec, per_seq(512), log_spec]
        + mask_specs
        + [pl.BlockSpec((HALF, queries_len), lambda at: (0, 0))] * 2,
        out_specs=[
            per_seq(query_cols),
            pl.BlockSpec((hi_n, queries_len, packed), lambda at: (0, at // (2 * seq_b), 0)),
        ],
        out_shape=[
            jax.ShapeDtypeStruct(slots + (query_cols,), jnp.bfloat16),
            jax.ShapeDtypeStruct((hi_n, CHIPS * local_len, packed), jnp.bfloat16),
        ],
        scratch_shapes=[pltpu.VMEM((seq_len, queries_len), jnp.float32), pair_scratch],
        compiler_params=params(),
        name="attend_back",
    )(
        queries, key_value, others, grad_mixed.reshape(slots + (512,)), log_total, *masks,
        cosine.T, sine_table.T,
    )
    final, others = dot_scatter(
        [after(active, gate_up_back)], [down_full], 3, (grad_key_value,)
    )
    result = shuffle((middle + final).astype(jnp.bfloat16), back)
    flat = (CHIPS, 2, seq_b, local_len)
    grad_qkv = pl.pallas_call(
        unrotate_kernel,
        grid=(CHIPS,),
        in_specs=[
            over_slots(query_cols),
            pl.BlockSpec((1, local_len, packed), lambda chip: (0, chip, 0)),
            pl.BlockSpec((hi_n - 1, local_len, packed), lambda chip: (0, chip, 0)),
            slot_table(),
            slot_table(),
        ],
        out_specs=over_slots(512),
        out_shape=jax.ShapeDtypeStruct(flat + (512,), jnp.bfloat16),
        compiler_params=params(),
        name="unrotate",
    )(
        after(grad_queries, final).reshape(flat + (query_cols,)),
        grad_key_value,
        others,
        cosine.reshape(place_shape + (HALF,)),
        sine_table.reshape(place_shape + (HALF,)),
    ).reshape(tokens, 512)
    heads_product = products(([normed_low, grad_branch], (0, 1)), [grad_qkv, mixed_rows])
    grad_norm_one = dot_scatter([after(grad_qkv, heads_product, down_back)], [qkv_full], 6)
    scaled_one = grad_norm_one * gain_one
    grad_input = grad_middle + inv_one * (
        scaled_one - normed_one * jnp.mean(scaled_one * normed_one, -1, keepdims=True)
    )
    head_grads = finish(from_group(sum_along(heads_product)))
    grad_query = head_grads[..., :query_cols].reshape(own_rows, -1)
    grad_key = head_grads[..., query_cols : query_cols + HEAD_DIM].reshape(own_rows, -1)
    grad_value = head_grads[..., query_cols + HEAD_DIM : qkv_cols].reshape(own_rows, -1)

    def gain_grad(gain, pairs):
        total = sum(jnp.sum(weight.astype(jnp.float32) * grad, 1) for weight, grad in pairs)
        return total / gain.astype(jnp.float32)

    attn_gain_grad = gain_grad(
        attn_gain,
        [(query_weight, grad_query), (key_weight, grad_key), (value_weight, grad_value)],
    )
    mlp_gain_grad = gain_grad(mlp_gain, [(gate_weight, gate_grads), (up_weight, up_grads)])
    return (
        result.reshape(seq_b, local_len, width),
        shuffle(grad_input, back).reshape(seq_b, local_len, width),
        attn_gain_grad,
        grad_query,
        grad_key,
        grad_value,
        head_grads[..., 512 : 512 + query_cols].reshape(own_rows, -1),
        mlp_gain_grad,
        gate_grads,
        up_grads,
        down_grads,
    )


def solution(mesh):
    y_n = mesh.shape["batch"] // 2
    lo_n = CHIPS // y_n
    hi_n = mesh.shape["seq"] // lo_n
    fine = Mesh(mesh.devices.reshape(y_n, 2, hi_n, lo_n), EVERY)
    token = P(("y", "core"), ("hi", "lo"), None)
    vector = P(EVERY)
    matrix = P(EVERY, None)
    in_specs = (
        token, vector, matrix, matrix, matrix, matrix, vector, matrix, matrix, matrix,
        P(("y", "core"), None), token,
    )
    out_specs = (
        token, token, vector, matrix, matrix, matrix, matrix, vector, matrix, matrix, matrix,
    )

    def run(*arrays):
        return shards((y_n, hi_n, lo_n), *arrays)

    return jax.shard_map(run, mesh=fine, in_specs=in_specs, out_specs=out_specs, check_vma=False)
```

```python
import functools
import math

import jax
import jax.numpy as jnp
from jax import lax
from jax.experimental import pallas as pl
from jax.experimental.pallas import tpu as pltpu
from jax.sharding import Mesh
from jax.sharding import PartitionSpec as P

HEADS = 32
KV_HEADS = 8
HEAD_DIM = 80
HALF = HEAD_DIM // 2
REPEAT = HEADS // KV_HEADS

EPSILON = 1e-05
ROPE_BASE = 10000.0

CHIPS = 4
SPLIT = 2 * CHIPS
OUT_COLS, QKV_COLS = 384, 512
GROUP = ("y", "core", "lo")
EVERY = ("y", "core", "hi", "lo")


def dot(left, right):
    return lax.dot_general(
        left, right, (((1,), (0,)), ((), ())), preferred_element_type=jnp.float32
    )


def by_columns(left, right):
    return lax.dot_general(
        left, right, (((1,), (1,)), ((), ())), preferred_element_type=jnp.float32
    )


def by_rows(left, right):
    return lax.dot_general(
        left, right, (((0,), (0,)), ((), ())), preferred_element_type=jnp.float32
    )


def swap(value, axis, step, size):
    return lax.ppermute(value, axis, [(place, place ^ step) for place in range(size)])


def to_group(weight):
    rows, cols = weight.shape[0], weight.shape[1] // SPLIT
    split = jnp.swapaxes(weight.reshape(rows, SPLIT, cols), 0, 1)
    return lax.all_to_all(split, GROUP, 0, 0, tiled=True).reshape(SPLIT * rows, cols)


def from_group(grads):
    rows, cols = grads.shape[0] // SPLIT, grads.shape[1]
    return lax.all_to_all(grads.reshape(SPLIT, rows, cols), GROUP, 0, 0, tiled=True)


def along(value):
    return lax.all_gather(value, "hi", axis=0, tiled=True)


def sum_along(value):
    return lax.psum_scatter(value, "hi", scatter_dimension=0, tiled=True)


MESH = pl.DeviceIdType.MESH
HALVES = 2


def places():
    chip = lax.axis_index("y") * lax.axis_size("lo") + lax.axis_index("lo")
    near = chip + 1 - 2 * lax.rem(chip, 2)
    return lax.axis_index("core"), (chip, near, lax.rem(chip + 2, CHIPS), CHIPS - 1 - chip)


def device_at(chip, core):
    lo_n = lax.axis_size("lo")
    return (lax.div(chip, lo_n), core, lax.axis_index("hi"), lax.rem(chip, lo_n))


def place_at(chip, core):
    lo_n = lax.axis_size("lo")
    return (lax.div(chip, lo_n) * 2 + core) * lo_n + lax.rem(chip, lo_n)


def peers():
    core, chips = places()
    return device_at(chips[0], 1 - core), device_at(chips[1], core), device_at(chips[2], core)


def along_hi(step):
    hi_n = lax.axis_size("hi")
    hi = lax.rem(lax.axis_index("hi") + step, hi_n)
    return lax.axis_index("y"), lax.axis_index("core"), hi, lax.axis_index("lo")


def exchange(source_of, dest_ref, zero_ref, send_sem, recv_sem, fill_sem):
    hi_n, hi = lax.axis_size("hi"), lax.axis_index("hi")
    parts = []
    for step in range(1, hi_n):
        copy = pltpu.make_async_remote_copy(
            src_ref=source_of(step),
            dst_ref=dest_ref.at[step - 1],
            send_sem=send_sem.at[step - 1],
            recv_sem=recv_sem.at[step - 1],
            device_id=along_hi(hi_n - step),
            device_id_type=MESH,
        )
        fill = pltpu.make_async_copy(zero_ref, dest_ref.at[step - 1], fill_sem.at[step - 1])
        parts.append((copy, fill, hi >= step, hi + step < hi_n))

    def start():
        zero_ref[...] = jnp.zeros_like(zero_ref)
        for copy, fill, sends, gets in parts:
            pl.when(sends)(copy.start)
            pl.when(jnp.logical_not(gets))(fill.start)

    def wait():
        for copy, fill, sends, gets in parts:
            pl.when(sends)(copy.wait_send)
            pl.when(gets)(copy.wait_recv)
            pl.when(jnp.logical_not(gets))(fill.wait)

    return start, wait


def relay(source_ref, dest_ref, zero_ref, send_sem, recv_sem, fill_sem):
    hi_n, hi = lax.axis_size("hi"), lax.axis_index("hi")
    copies, fills = [], []
    for step in range(1, hi_n):
        copies.append(
            pltpu.make_async_remote_copy(
                src_ref=source_ref if step == 1 else dest_ref.at[step - 2],
                dst_ref=dest_ref.at[step - 1],
                send_sem=send_sem.at[step - 1],
                recv_sem=recv_sem.at[step - 1],
                device_id=along_hi(1),
                device_id_type=MESH,
            )
        )
        fills.append(pltpu.make_async_copy(zero_ref, dest_ref.at[step - 1], fill_sem.at[step - 1]))

    def sends(step):
        return jnp.logical_and(hi + 1 < hi_n, hi >= step - 1)

    def start():
        zero_ref[...] = jnp.zeros_like(zero_ref)
        for step in range(1, hi_n):
            pl.when(hi < step)(fills[step - 1].start)
        pl.when(sends(1))(copies[0].start)

    def run():
        for step in range(1, hi_n):
            pl.when(hi >= step)(copies[step - 1].wait_recv)
            if step + 1 < hi_n:
                pl.when(sends(step + 1))(copies[step].start)
        for step in range(1, hi_n):
            pl.when(sends(step))(copies[step - 1].wait_send)
            pl.when(hi < step)(fills[step - 1].wait)

    return start, run


def turn_scratch(shape, dtype, others):
    return [pltpu.VMEM(shape, dtype)] + [pltpu.SemaphoreType.DMA((others,))] * 3


def meet(devices):
    barrier = pltpu.get_barrier_semaphore()
    for device in devices:
        pl.semaphore_signal(barrier, inc=1, device_id=device, device_id_type=MESH)
    pl.semaphore_wait(barrier, len(devices))


def gather_dot_kernel(weights_n, gated, starts, *refs):
    refs = list(refs)

    def take(count):
        taken = refs[:count]
        del refs[:count]
        return taken

    outs_n = 3 if gated else weights_n
    (x_ref,) = take(1)
    weight_refs = take(weights_n)
    (all_ref,) = take(1)
    out_refs = take(outs_n)
    (x_buf,) = take(1)
    weight_bufs = take(weights_n)
    out_bufs = take(outs_n)
    load_sem, weight_sem, keep_sem, out_sem, send_sem, recv_sem = refs
    core_peer, near_peer, far_peer = peers()
    rows = x_ref.shape[0]
    half = rows // HALVES

    def piece(ref, at):
        return ref.at[pl.ds(at * half, half)]

    def route(index, source, step, core, device, halves=range(HALVES)):
        return [
            pltpu.make_async_remote_copy(
                src_ref=piece(source, at),
                dst_ref=piece(x_buf.at[step, core], at),
                send_sem=send_sem.at[index, at],
                recv_sem=recv_sem.at[index, at],
                device_id=device,
                device_id_type=MESH,
            )
            for at in halves
        ]

    to_near = route(0, x_ref, 1, 0, near_peer)
    to_far = route(1, x_ref, 2, 0, far_peer)
    to_core = route(2, x_ref, 0, 1, core_peer)
    onward = [
        *route(3, x_buf.at[2, 0], 3, 0, near_peer, (0,)),
        *route(3, x_buf.at[1, 0], 3, 0, far_peer, (1,)),
    ]
    near_core = route(4, x_buf.at[1, 0], 1, 1, core_peer)
    far_core = route(5, x_buf.at[2, 0], 2, 1, core_peer)
    onward_core = route(6, x_buf.at[3, 0], 3, 1, core_peer)

    load = pltpu.make_async_copy(x_ref, x_buf.at[0, 0], load_sem)
    load.start()
    fetches = []
    for at in range(weights_n):
        columns = pl.ds(starts[at], weight_bufs[at].shape[1])
        fetch = pltpu.make_async_copy(
            weight_refs[at].at[:, columns], weight_bufs[at], weight_sem.at[at]
        )
        fetch.start()
        fetches.append(fetch)
    meet((core_peer, near_peer, far_peer))
    for copy in (to_near[1], to_far[0], to_near[0], to_far[1], to_core[0], to_core[1]):
        copy.start()
    kept, stored = [], []

    def keep(step, core):
        copy = pltpu.make_async_copy(
            x_buf.at[step, core], all_ref.at[step, core], keep_sem.at[step, core]
        )
        copy.start()
        kept.append(copy)

    def compute(step, core):
        turn = len(stored) % 2
        if len(stored) >= 2:
            for copy in stored[-2]:
                copy.wait()
        values = [dot(x_buf[step, core], buf[...]) for buf in weight_bufs]
        if gated:
            gate, up = values
            values = [gate, up, gate / (1.0 + jnp.exp(-gate)) * up]
        copies = []
        for at, value in enumerate(values):
            out_bufs[at][turn] = value.astype(out_bufs[at].dtype)
            copy = pltpu.make_async_copy(
                out_bufs[at].at[turn], out_refs[at].at[step, core], out_sem.at[at, turn]
            )
            copy.start()
            copies.append(copy)
        stored.append(copies)

    load.wait()
    keep(0, 0)
    for fetch in fetches:
        fetch.wait()
    compute(0, 0)
    for at in range(HALVES):
        to_core[at].wait_recv()
    keep(0, 1)
    compute(0, 1)
    to_far[0].wait_recv()
    onward[0].start()
    far_core[0].start()
    to_near[1].wait_recv()
    onward[1].start()
    near_core[1].start()
    to_far[1].wait_recv()
    far_core[1].start()
    to_near[0].wait_recv()
    near_core[0].start()
    keep(2, 0)
    keep(1, 0)
    compute(2, 0)
    compute(1, 0)
    for step, copies in ((2, far_core), (1, near_core)):
        for at in range(HALVES):
            copies[at].wait_recv()
        keep(step, 1)
        compute(step, 1)
    for at in range(HALVES):
        onward[at].wait_recv()
        onward_core[at].start()
    keep(3, 0)
    compute(3, 0)
    for at in range(HALVES):
        onward_core[at].wait_recv()
    keep(3, 1)
    compute(3, 1)
    for copies in (to_near, to_far, to_core, onward, near_core, far_core, onward_core):
        for copy in copies:
            copy.wait_send()
    for copy in kept:
        copy.wait()
    for copies in stored[-2:]:
        for copy in copies:
            copy.wait()


def gather_dot(value, weights, dtypes, collective_id, gated=False, windows=None):
    rows, width = value.shape
    windows = windows or [(0, weight.shape[1]) for weight in weights]
    cols = [count for start, count in windows]
    out_cols = cols[:1] * 3 if gated else cols
    flops = 2 * SPLIT * rows * width * sum(cols)
    anywhere = pl.BlockSpec(memory_space=pl.ANY)
    return pl.pallas_call(
        functools.partial(gather_dot_kernel, len(weights), gated, [at for at, count in windows]),
        in_specs=[anywhere] * (1 + len(weights)),
        out_specs=[anywhere] * (1 + len(out_cols)),
        out_shape=[jax.ShapeDtypeStruct((CHIPS, 2, rows, width), value.dtype)]
        + [
            jax.ShapeDtypeStruct((CHIPS, 2, rows, count), dtype)
            for count, dtype in zip(out_cols, dtypes)
        ],
        scratch_shapes=[pltpu.VMEM((CHIPS, 2, rows, width), value.dtype)]
        + [pltpu.VMEM((width, count), jnp.bfloat16) for count in cols]
        + [pltpu.VMEM((2, rows, count), dtype) for count, dtype in zip(out_cols, dtypes)]
        + [
            pltpu.SemaphoreType.DMA,
            pltpu.SemaphoreType.DMA((len(weights),)),
            pltpu.SemaphoreType.DMA((CHIPS, 2)),
            pltpu.SemaphoreType.DMA((len(out_cols), 2)),
            pltpu.SemaphoreType.DMA((7, HALVES)),
            pltpu.SemaphoreType.DMA((7, HALVES)),
        ],
        compiler_params=pltpu.CompilerParams(
            vmem_limit_bytes=60 << 20, collective_id=collective_id, has_side_effects=True
        ),
        cost_estimate=pl.CostEstimate(
            flops=flops // 4, bytes_accessed=SPLIT * rows * width * 4, transcendentals=0
        ),
        name=f"gather_dot_{collective_id}",
    )(value, *weights)


def hosted(uses, left_refs, right_refs, out_ref, *scratch):
    right_bufs, (left_buf, out_buf, right_sem, left_sem, out_sem) = (
        scratch[: len(uses)],
        scratch[len(uses) :],
    )
    block = left_buf.shape[3]
    count = out_ref.shape[0] // block
    loads = [
        pltpu.make_async_copy(ref, buf, right_sem.at[at])
        for at, (ref, buf) in enumerate(zip(right_refs, right_bufs))
    ]

    def fetch(at, slot):
        columns = pl.ds(pl.multiple_of(at * block, block), block)
        return [
            pltpu.make_async_copy(
                ref.at[:, columns], left_buf.at[slot, index], left_sem.at[slot, index]
            )
            for index, ref in enumerate(left_refs)
        ]

    def store(at, slot):
        rows = pl.ds(pl.multiple_of(at * block, block), block)
        return pltpu.make_async_copy(out_buf.at[slot], out_ref.at[rows], out_sem.at[slot])

    def start():
        for copy in loads + fetch(0, 0):
            copy.start()

    def run():
        for copy in loads:
            copy.wait()

        def body(at, carry):
            slot = lax.rem(at, 2)

            @pl.when(at + 1 < count)
            def _():
                for copy in fetch(at + 1, 1 - slot):
                    copy.start()

            for copy in fetch(at, slot):
                copy.wait()
            pl.when(at >= 2)(lambda: store(at - 2, slot).wait())
            column = 0
            for index, buf in zip(uses, right_bufs):
                value = by_rows(left_buf[slot, index], buf[...])
                out_buf[slot, :, column : column + buf.shape[1]] = value.astype(jnp.bfloat16)
                column += buf.shape[1]
            store(at, slot).start()
            return carry

        lax.fori_loop(0, count, body, 0)
        for at in (count - 2, count - 1):
            store(at, at % 2).wait()

    return start, run


def dot_scatter_kernel(lefts_n, parts_n, extra, starts, uses, *refs):
    refs = list(refs)

    def take(count):
        taken = refs[:count]
        del refs[:count]
        return taken

    left_refs = take(lefts_n)
    weight_refs = take(lefts_n)
    extra_ref = take(extra)
    host_lefts = take(max(uses) + 1 if uses else 0)
    host_rights = take(len(uses))
    (out_ref,) = take(1)
    extra_out = take(extra)
    host_out = take(1 if uses else 0)
    left_bufs = take(lefts_n)
    weight_bufs = take(lefts_n)
    core_out, core_in, chip_out, chip_in = take(4)
    left_sem, weight_sem, core_send, core_recv, chip_send, chip_recv = take(6)
    core_peer, near_peer, far_peer = peers()
    rows = left_refs[0].shape[2]
    cols = weight_refs[0].shape[0] // parts_n
    tile = 256 if cols % 256 == 0 else 128
    order = (3, 1, 2, 0)

    fetches = {}
    for part in range(parts_n):
        for at in range(lefts_n):
            fetches["weight", part, at] = pltpu.make_async_copy(
                weight_refs[at].at[
                    pl.ds(part * cols, cols), pl.ds(starts[at], weight_bufs[at].shape[1])
                ],
                weight_bufs[at].at[pl.ds(part * cols, cols)],
                weight_sem.at[at, part],
            )
    for step in order:
        for core in (1, 0):
            for at in range(lefts_n):
                fetches[step, core, at] = pltpu.make_async_copy(
                    left_refs[at].at[step, core],
                    left_bufs[at].at[step, core],
                    left_sem.at[at, step, core],
                )
    for at in range(lefts_n):
        fetches["weight", 0, at].start()
    for step in order[:1]:
        for core in (1, 0):
            for at in range(lefts_n):
                fetches[step, core, at].start()
    for part in range(1, parts_n):
        for at in range(lefts_n):
            fetches["weight", part, at].start()
    for step in order[1:]:
        for core in (1, 0):
            for at in range(lefts_n):
                fetches[step, core, at].start()
    hi_n = lax.axis_size("hi")
    meet([core_peer, near_peer, far_peer] + [along_hi(step) for step in range(1, hi_n) if extra])
    if extra:
        start_turns, wait_turns = exchange(
            lambda step: extra_ref[0].at[step], extra_out[0], *take(4)
        )
        start_turns()
    if uses:
        start_host, run_host = hosted(uses, host_lefts, host_rights, host_out[0], *take(len(uses) + 5))
        start_host()
    waited = set()

    def ready(*key):
        for at in range(lefts_n):
            if key + (at,) not in waited:
                waited.add(key + (at,))
                fetches[key + (at,)].wait()

    def product(step, core, part, place):
        total = None
        for left, weight in zip(left_bufs, weight_bufs):
            at = pl.multiple_of(part * cols + place * tile, tile)
            term = by_columns(left[step, core], weight[pl.ds(at, tile)])
            total = term if total is None else total + term
        return total

    def wide(part, place):
        return pl.ds(pl.multiple_of(part * cols + place * tile, tile), tile)

    def each_tile(body):
        def run(place, carry):
            body(place, pl.ds(pl.multiple_of(place * tile, tile), tile))
            return carry

        lax.fori_loop(0, cols // tile, run, 0)

    def core_copy(step, part):
        return pltpu.make_async_remote_copy(
            src_ref=core_out.at[step, part],
            dst_ref=core_in.at[step, part],
            send_sem=core_send.at[step, part],
            recv_sem=core_recv.at[step, part],
            device_id=core_peer,
            device_id_type=MESH,
        )

    def chip_copy(step, part):
        return pltpu.make_async_remote_copy(
            src_ref=chip_out.at[step - 1, part],
            dst_ref=chip_in.at[step - 1, part],
            send_sem=chip_send.at[step - 1, part],
            recv_sem=chip_recv.at[step - 1, part],
            device_id=far_peer if step == 2 or (step == 3 and part % 2) else near_peer,
            device_id_type=MESH,
        )

    def joint(part):
        return 1 if part % 2 else 2

    def other_core(step, part):
        ready("weight", part)
        ready(step, 1)

        def body(place, columns):
            core_out[step, part, :, columns] = product(step, 1, part, place).astype(jnp.bfloat16)

        each_tile(body)
        core_copy(step, part).start()

    def this_core(step, part):
        ready(step, 0)
        core_copy(step, part).wait_recv()
        joins = step == joint(part)
        if joins:
            chip_copy(3, part).wait_recv()

        def body(place, columns):
            total = product(step, 0, part, place)
            total += core_in[step, part, :, columns].astype(jnp.float32)
            if joins:
                total += chip_in[2, part, :, columns].astype(jnp.float32)
            if step:
                chip_out[step - 1, part, :, columns] = total.astype(jnp.bfloat16)
            else:
                out_ref[:, wide(part, place)] = total

        each_tile(body)
        if step:
            chip_copy(step, part).start()

    parts = range(parts_n)
    for part in parts:
        other_core(3, part)
    for part in parts:
        this_core(3, part)
    for part in parts:
        other_core(3 - joint(part), part)
    for part in parts:
        this_core(3 - joint(part), part)
    for part in parts:
        other_core(joint(part), part)
        other_core(0, part)
    for part in parts:
        this_core(0, part)
    for part in parts:
        this_core(joint(part), part)
    if uses:
        run_host()
    for step in (1, 2):
        for part in parts:
            chip_copy(step, part).wait_recv()
            columns = pl.ds(part * cols, cols)
            out_ref[:, columns] += chip_in[step - 1, part].astype(jnp.float32)
    for part in parts:
        for step in range(CHIPS):
            core_copy(step, part).wait_send()
            if step:
                chip_copy(step, part).wait_send()
    if extra:
        wait_turns()


def dot_scatter(lefts, weights, collective_id, extra=(), windows=None, host=((), (), ())):
    windows = windows or [(0, weight.shape[1]) for weight in weights]
    host_lefts, uses, host_rights = host
    total = sum(right.shape[1] for right in host_rights)
    block = 256
    others = lax.axis_size("hi") - 1
    lefts = [left.reshape(CHIPS, 2, left.size // (SPLIT * left.shape[-1]), left.shape[-1]) for left in lefts]
    rows = lefts[0].shape[2]
    parts_n = 2
    cols = weights[0].shape[0] // parts_n
    depths = [left.shape[3] for left in lefts]
    flops = 2 * SPLIT * rows * cols * parts_n * sum(depths)
    anywhere = pl.BlockSpec(memory_space=pl.ANY)
    out, *received = pl.pallas_call(
        functools.partial(
            dot_scatter_kernel, len(lefts), parts_n, len(extra), [at for at, count in windows], uses
        ),
        in_specs=[anywhere]
        * (2 * len(lefts) + len(extra) + len(host_lefts) + len(host_rights)),
        out_specs=[pl.BlockSpec(memory_space=pltpu.VMEM)]
        + [anywhere] * (len(extra) + bool(uses)),
        out_shape=[jax.ShapeDtypeStruct((rows, parts_n * cols), jnp.float32)]
        + [jax.ShapeDtypeStruct((others,) + array.shape[1:], array.dtype) for array in extra]
        + [jax.ShapeDtypeStruct((parts_n * cols, total), jnp.bfloat16)] * bool(uses),
        scratch_shapes=[pltpu.VMEM((CHIPS, 2, rows, depth), jnp.bfloat16) for depth in depths]
        + [pltpu.VMEM((parts_n * cols, depth), jnp.bfloat16) for depth in depths]
        + [
            pltpu.VMEM((CHIPS, parts_n, rows, cols), jnp.bfloat16),
            pltpu.VMEM((CHIPS, parts_n, rows, cols), jnp.bfloat16),
            pltpu.VMEM((CHIPS - 1, parts_n, rows, cols), jnp.bfloat16),
            pltpu.VMEM((CHIPS - 1, parts_n, rows, cols), jnp.bfloat16),
            pltpu.SemaphoreType.DMA((len(lefts), CHIPS, 2)),
            pltpu.SemaphoreType.DMA((len(lefts), parts_n)),
            pltpu.SemaphoreType.DMA((CHIPS, parts_n)),
            pltpu.SemaphoreType.DMA((CHIPS, parts_n)),
            pltpu.SemaphoreType.DMA((CHIPS - 1, parts_n)),
            pltpu.SemaphoreType.DMA((CHIPS - 1, parts_n)),
        ]
        + [
            scratch
            for array in extra
            for scratch in turn_scratch(array.shape[1:], array.dtype, others)
        ]
        + [pltpu.VMEM(right.shape, right.dtype) for right in host_rights]
        + [
            pltpu.VMEM((2, len(host_lefts)) + (SPLIT * rows, block), jnp.bfloat16),
            pltpu.VMEM((2, block, total), jnp.bfloat16),
            pltpu.SemaphoreType.DMA((len(uses),)),
            pltpu.SemaphoreType.DMA((2, len(host_lefts))),
            pltpu.SemaphoreType.DMA((2,)),
        ]
        * bool(uses),
        compiler_params=pltpu.CompilerParams(
            vmem_limit_bytes=60 << 20, collective_id=collective_id, has_side_effects=True
        ),
        cost_estimate=pl.CostEstimate(
            flops=flops // 4, bytes_accessed=SPLIT * rows * cols * parts_n * 4, transcendentals=0
        ),
        name=f"dot_scatter_{collective_id}",
    )(*lefts, *weights, *extra, *host_lefts, *host_rights)
    return (out, *received) if received else out


def shuffle_kernel(order, piece, x_ref, out_ref):
    rows = x_ref[...]
    out_ref[...] = jnp.concatenate([rows[:, at * piece : (at + 1) * piece] for at in order], 1)


def shuffle(value, order):
    rows, width = value.shape
    return pl.pallas_call(
        functools.partial(shuffle_kernel, order, width // len(order)),
        out_shape=jax.ShapeDtypeStruct(value.shape, value.dtype),
        compiler_params=params(),
        name="shuffle",
    )(value)


def products_kernel(left_ref, *refs):
    left = left_ref[...]
    for right_ref, out_ref in zip(refs[: len(refs) // 2], refs[len(refs) // 2 :]):
        out_ref[...] = by_rows(left, right_ref[...]).astype(jnp.bfloat16)


def products(left, rights, block=256):
    tokens, width = left.shape
    cols = [right.shape[1] for right in rights]
    return pl.pallas_call(
        products_kernel,
        grid=(width // block,),
        in_specs=[pl.BlockSpec((tokens, block), lambda at: (0, at))]
        + [
            pl.BlockSpec((tokens, count), lambda at: (0, 0), pipeline_mode=pl.Buffered(1))
            for count in cols
        ],
        out_specs=[pl.BlockSpec((block, count), lambda at: (at, 0)) for count in cols],
        out_shape=[jax.ShapeDtypeStruct((width, count), jnp.bfloat16) for count in cols],
        compiler_params=params(),
        cost_estimate=pl.CostEstimate(
            flops=4 * tokens * width * sum(cols), bytes_accessed=2 * tokens * width, transcendentals=0
        ),
        name="products",
    )(left, *rights)


def project_kernel(
    x_ref, gain_ref, weight_ref, cosine_ref, sine_ref, low_ref, query_ref, key_value_ref
):
    source = x_ref[...].astype(jnp.float32)
    inverse = lax.rsqrt(jnp.mean(source * source, -1, keepdims=True) + EPSILON)
    low_ref[...] = (source * inverse * gain_ref[...]).astype(jnp.bfloat16)
    rows = dot(low_ref[...], weight_ref[:, OUT_COLS:])
    count = rows.shape[0] // cosine_ref.shape[1]
    cosine = jnp.concatenate([cosine_ref[0]] * count, 0)
    sine_table = jnp.concatenate([sine_ref[0]] * count, 0)
    turned = []
    for values in heads_of(rows, REPEAT + 1):
        first_half, second_half = values[:, :HALF], values[:, HALF:]
        turned += [
            first_half * cosine - second_half * sine_table,
            second_half * cosine + first_half * sine_table,
        ]
    query_ref[...] = jnp.concatenate(turned[: 2 * REPEAT], 1).astype(jnp.bfloat16)
    value = rows[:, HEAD_DIM * (REPEAT + 1) : HEAD_DIM * (REPEAT + 2)]
    both = jnp.concatenate(turned[2 * REPEAT :] + [value], 1).astype(jnp.bfloat16)
    length = cosine_ref.shape[1]
    key_value_ref[...] = jnp.concatenate(
        [both[length * at : length * (at + 1)] for at in range(count)], 1
    )


def spread_kernel(weights_n, extra, *refs):
    refs = list(refs)

    def take(count):
        taken = refs[:count]
        del refs[:count]
        return taken

    (x_ref,), weight_refs, extra_ref = take(1), take(weights_n), take(extra)
    (all_ref,), group_refs, extra_out = take(1), take(weights_n), take(extra)
    local_sem, send_sem, recv_sem, spread_send, spread_recv = take(5)
    core_peer, near_peer, far_peer = peers()
    core, chips = places()
    cols = group_refs[0].shape[2]
    own_place = place_at(chips[0], core)

    half = x_ref.shape[0] // HALVES

    def route(index, source, step, to_core, device, halves=range(HALVES)):
        return [
            pltpu.make_async_remote_copy(
                src_ref=source.at[pl.ds(at * half, half)],
                dst_ref=all_ref.at[step, to_core, pl.ds(at * half, half)],
                send_sem=send_sem.at[index, at],
                recv_sem=recv_sem.at[index, at],
                device_id=device,
                device_id_type=MESH,
            )
            for at in halves
        ]

    to_near = route(0, x_ref, 1, 0, near_peer)
    to_far = route(1, x_ref, 2, 0, far_peer)
    to_core = route(2, x_ref, 0, 1, core_peer)
    onward = [
        *route(3, all_ref.at[2, 0], 3, 0, near_peer, (0,)),
        *route(3, all_ref.at[1, 0], 3, 0, far_peer, (1,)),
    ]
    near_core = route(4, all_ref.at[1, 0], 1, 1, core_peer)
    far_core = route(5, all_ref.at[2, 0], 2, 1, core_peer)
    onward_core = route(6, all_ref.at[3, 0], 3, 1, core_peer)
    own = pltpu.make_async_copy(x_ref, all_ref.at[0, 0], local_sem.at[weights_n])
    own.start()
    mine = []
    for at in range(weights_n):
        columns = pl.ds(pl.multiple_of(own_place * cols, 128), cols)
        copy = pltpu.make_async_copy(
            weight_refs[at].at[:, columns], group_refs[at].at[own_place], local_sem.at[at]
        )
        copy.start()
        mine.append(copy)
    others = [(step, flip) for step in range(CHIPS) for flip in range(2)][1:]
    devices = [device_at(chips[step], 1 - core if flip else core) for step, flip in others]
    hi_n = lax.axis_size("hi")
    meet(devices + [along_hi(step) for step in range(1, hi_n) if extra])
    if extra:
        start_turns, wait_turns = relay(extra_ref[0], extra_out[0], *take(4))
        start_turns()
    for copy in (to_near[1], to_far[0], to_near[0], to_far[1], to_core[0], to_core[1]):
        copy.start()
    copies = []
    for at in range(weights_n):
        for index, (step, flip) in enumerate(others):
            place = place_at(chips[step], 1 - core if flip else core)
            columns = pl.ds(pl.multiple_of(place * cols, 128), cols)
            copies.append(
                pltpu.make_async_remote_copy(
                    src_ref=weight_refs[at].at[:, columns],
                    dst_ref=group_refs[at].at[own_place],
                    send_sem=spread_send.at[at, index],
                    recv_sem=spread_recv.at[at, index],
                    device_id=devices[index],
                    device_id_type=MESH,
                )
            )
    to_far[0].wait_recv()
    onward[0].start()
    far_core[0].start()
    to_near[1].wait_recv()
    onward[1].start()
    near_core[1].start()
    to_far[1].wait_recv()
    far_core[1].start()
    to_near[0].wait_recv()
    near_core[0].start()
    for copy in copies:
        copy.start()
    for at in range(HALVES):
        onward[at].wait_recv()
        onward_core[at].start()
    for group in (near_core, far_core, to_core, onward_core):
        for copy in group:
            copy.wait_recv()
    for group in (to_near, to_far, to_core, onward, near_core, far_core, onward_core):
        for copy in group:
            copy.wait_send()
    if extra:
        wait_turns()
    for copy in copies:
        copy.wait()
    for copy in mine:
        copy.wait()
    own.wait()


def spread_and_gather(value, weights, collective_id, extra=()):
    others = lax.axis_size("hi") - 1
    rows, width = value.shape
    own_rows, cols = weights[0].shape[0], weights[0].shape[1] // SPLIT
    anywhere = pl.BlockSpec(memory_space=pl.ANY)
    count = len(weights)
    gathered, *groups = pl.pallas_call(
        functools.partial(spread_kernel, count, len(extra)),
        in_specs=[anywhere] * (1 + count + len(extra)),
        out_specs=[anywhere] * (1 + count + len(extra)),
        out_shape=[jax.ShapeDtypeStruct((CHIPS, 2, rows, width), value.dtype)]
        + [jax.ShapeDtypeStruct((SPLIT, own_rows, cols), jnp.bfloat16)] * count
        + [jax.ShapeDtypeStruct((others,) + array.shape, array.dtype) for array in extra],
        scratch_shapes=[
            pltpu.SemaphoreType.DMA((count + 1,)),
            pltpu.SemaphoreType.DMA((7, HALVES)),
            pltpu.SemaphoreType.DMA((7, HALVES)),
            pltpu.SemaphoreType.DMA((count, SPLIT - 1)),
            pltpu.SemaphoreType.DMA((count, SPLIT - 1)),
        ]
        + [scratch for array in extra for scratch in turn_scratch(array.shape, array.dtype, others)],
        compiler_params=pltpu.CompilerParams(
            vmem_limit_bytes=60 << 20, collective_id=collective_id, has_side_effects=True
        ),
        cost_estimate=pl.CostEstimate(
            flops=10**9, bytes_accessed=SPLIT * rows * width * 4, transcendentals=0
        ),
        name=f"spread_{collective_id}",
    )(value, *weights, *extra)
    groups[:count] = [group.reshape(SPLIT * own_rows, cols) for group in groups[:count]]
    return gathered, *groups


def after(value, *others):
    return lax.optimization_barrier((value,) + others)[0]


def by_step(value, at, axis):
    steps = [
        lax.dynamic_index_in_dim(value, at ^ step, axis) for step in range(value.shape[axis])
    ]
    return jnp.concatenate(steps, axis)


def params(limit=60):
    return pltpu.CompilerParams(vmem_limit_bytes=limit << 20)


def heads_of(values, count):
    return [values[:, HEAD_DIM * at : HEAD_DIM * (at + 1)] for at in range(count)]


def allow(key_seg_ref, key_place_ref, query_seg_ref, query_place_ref):
    allowed = (key_seg_ref[0] == query_seg_ref[0]) & (key_place_ref[...] <= query_place_ref[...])
    return jnp.where(allowed, 0.0, -1e30).T


def unpack(own_ref, others_ref, pair_ref):
    pair, length = 2 * HEAD_DIM, own_ref.shape[0]
    count = own_ref.shape[1] // pair
    for case in range(count):

        @pl.when(pl.program_id(0) % count == case)
        def _():
            columns = slice(pair * case, pair * (case + 1))
            pair_ref[:length] = own_ref[:, columns]
            for step in range(others_ref.shape[0]):
                pair_ref[length * (step + 1) : length * (step + 2)] = others_ref[step, :, columns]


def attend_kernel(
    query_ref, own_ref, others_ref, key_seg_ref, key_place_ref, query_seg_ref, query_place_ref,
    mixed_ref, log_ref, bias_ref, pair_ref,
):
    queries_len = query_seg_ref.shape[1]
    seq_len = key_seg_ref.shape[2]
    to_log2 = 1.0 / math.sqrt(HEAD_DIM) / math.log(2.0)
    bias_ref[...] = allow(key_seg_ref, key_place_ref, query_seg_ref, query_place_ref)
    rows = query_ref[0, :, 0, 0].reshape(queries_len, REPEAT * HEAD_DIM)
    unpack(own_ref, others_ref, pair_ref)
    key_rows, value_rows = heads_of(pair_ref[...], 2)
    mixed = []
    for at, query_rows in enumerate(heads_of(rows, REPEAT)):
        scores = by_columns(key_rows, query_rows) * to_log2 + bias_ref[...]
        highest = jnp.max(scores, 0, keepdims=True)
        weight = jnp.exp2(scores - highest)
        total = jnp.sum(weight, 0, keepdims=True)
        probabilities = (weight * (1.0 / total)).astype(jnp.bfloat16)
        mixed.append(by_rows(value_rows, probabilities).T)
        log_ref[0, at : at + 1] = highest + jnp.log2(total)
    mixed.append(jnp.zeros((queries_len, mixed_ref.shape[5] - REPEAT * HEAD_DIM), jnp.float32))
    mixed = jnp.concatenate(mixed, 1).astype(jnp.bfloat16)
    mixed_ref[0, :, 0, 0] = mixed.reshape(mixed_ref.shape[1], mixed_ref.shape[4], mixed.shape[1])


def attend_back_kernel(
    query_ref, own_ref, others_ref, grad_ref, log_ref, key_seg_ref, key_place_ref, query_seg_ref,
    query_place_ref, cosine_ref, sine_ref, grad_query_ref, grad_key_value_ref, bias_ref, pair_ref,
):
    queries_len = query_seg_ref.shape[1]
    seq_len = key_seg_ref.shape[2]
    scaling = 1.0 / math.sqrt(HEAD_DIM)
    to_log2 = scaling / math.log(2.0)
    bias_ref[...] = allow(key_seg_ref, key_place_ref, query_seg_ref, query_place_ref)
    query_rows = query_ref[0, :, 0, 0].reshape(queries_len, REPEAT * HEAD_DIM)
    grad_rows = grad_ref[0, :, 0, 0].reshape(queries_len, grad_ref.shape[5])
    unpack(own_ref, others_ref, pair_ref)
    key_rows, value_rows = heads_of(pair_ref[...], 2)
    cosine, sine_table = cosine_ref[...], sine_ref[...]
    grad_keys = jnp.zeros((seq_len, HEAD_DIM), jnp.float32)
    grad_values = jnp.zeros((seq_len, HEAD_DIM), jnp.float32)
    grad_queries = []
    for at in range(REPEAT):
        query, grad = heads_of(query_rows, REPEAT)[at], heads_of(grad_rows, REPEAT)[at]
        scores = by_columns(key_rows, query) * to_log2 + bias_ref[...]
        probabilities = jnp.exp2(scores - log_ref[0, at : at + 1])
        grad_probs = by_columns(value_rows, grad)
        centre = jnp.sum(probabilities * grad_probs, 0, keepdims=True)
        grad_scores = (probabilities * (grad_probs - centre)).astype(jnp.bfloat16)
        grad_values += dot(probabilities.astype(jnp.bfloat16), grad)
        grad_keys += dot(grad_scores, query)
        turned = by_rows(key_rows, grad_scores) * scaling
        first_half, second_half = turned[:HALF], turned[HALF:]
        turned = jnp.concatenate(
            [
                first_half * cosine + second_half * sine_table,
                second_half * cosine - first_half * sine_table,
            ],
            0,
        )
        grad_queries.append(turned.T)
    grad_queries = jnp.concatenate(grad_queries, 1).astype(jnp.bfloat16)
    grad_query_ref[0, :, 0, 0] = grad_queries.reshape(
        grad_query_ref.shape[1], grad_query_ref.shape[4], grad_queries.shape[1]
    )
    both = jnp.concatenate([grad_keys * scaling, grad_values], 1).astype(jnp.bfloat16)
    both = both.reshape(grad_key_value_ref.shape[0], queries_len, 2 * HEAD_DIM)
    count = grad_key_value_ref.shape[2] // (2 * HEAD_DIM)
    for case in range(count):

        @pl.when(pl.program_id(0) % count == case)
        def _():
            columns = slice(2 * HEAD_DIM * case, 2 * HEAD_DIM * (case + 1))
            grad_key_value_ref[:, :, columns] = both


def unrotate_kernel(grad_query_ref, own_ref, others_ref, cosine_ref, sine_ref, grad_ref):
    cosine, sine_table = cosine_ref[0], sine_ref[0]
    total = own_ref[0].astype(jnp.float32)
    for step in range(others_ref.shape[0]):
        total += others_ref[step].astype(jnp.float32)
    for at in range(grad_ref.shape[1] * grad_ref.shape[2]):
        place = (0, at // grad_ref.shape[2], at % grad_ref.shape[2])
        rows = total[:, 2 * HEAD_DIM * at : 2 * HEAD_DIM * (at + 1)]
        first_half, second_half = rows[:, :HALF], rows[:, HALF:HEAD_DIM]
        turned = jnp.concatenate(
            [
                first_half * cosine + second_half * sine_table,
                second_half * cosine - first_half * sine_table,
                rows[:, HEAD_DIM:],
                jnp.zeros((rows.shape[0], grad_ref.shape[4] - (REPEAT + 2) * HEAD_DIM), jnp.float32),
            ],
            1,
        ).astype(jnp.bfloat16)
        grad_ref[place] = jnp.concatenate([grad_query_ref[place], turned], 1)


def shards(
    sizes,
    hidden_in,
    attn_gain,
    query_weight,
    key_weight,
    value_weight,
    out_weight,
    mlp_gain,
    gate_weight,
    up_weight,
    down_weight,
    segment_ids,
    grad_output,
):
    y_n, hi_n, lo_n = sizes
    seq_b, local_len, width = hidden_in.shape
    seq_len = segment_ids.shape[1]
    rows = seq_b * local_len
    tokens = SPLIT * rows
    own_rows = query_weight.shape[0]
    ff_width = gate_weight.shape[1]
    ff_pad = -(-ff_width // (SPLIT * 128)) * SPLIT * 128
    query_cols = HEADS * HEAD_DIM // SPLIT
    qkv_cols = query_cols + 2 * HEAD_DIM
    y_at, core_at = lax.axis_index("y"), lax.axis_index("core")
    hi_at, lo_at = lax.axis_index("hi"), lax.axis_index("lo")

    pieces = [(outer, at) for at in range(hi_n) for outer in range(2 * y_n)]
    order = [outer * hi_n + at for outer, at in pieces]
    back = [order.index(at) for at in range(len(order))]

    def spread(*groups):
        pieces = []
        for group, total in zip(groups[::2], groups[1::2]):
            pieces += [piece.reshape(own_rows, SPLIT, -1) for piece in group]
            empty = total - sum(piece.size // (own_rows * SPLIT) for piece in group)
            if empty:
                pieces.append(jnp.zeros((own_rows, SPLIT, empty), jnp.bfloat16))
        return to_group(jnp.concatenate(pieces, -1).reshape(own_rows, -1))

    def widen(weight):
        return jnp.pad(weight, ((0, 0), (0, ff_pad - ff_width)))

    def everywhere(weight):
        return along(weight)

    first_group = spread([out_weight], OUT_COLS, [query_weight, key_weight, value_weight], QKV_COLS)
    offset = (hi_at * lo_n + lo_at) * local_len
    own_segments = lax.dynamic_slice_in_dim(segment_ids, offset, local_len, 1)
    small = jnp.concatenate(
        [attn_gain, mlp_gain, own_segments.astype(jnp.bfloat16).reshape(rows)]
    )
    small = after(small, first_group)
    small_pad = -(-small.shape[0] // 128) * 128
    small = jnp.pad(small, (0, small_pad - small.shape[0])).reshape(1, 1, 1, 1, small_pad)
    for axis, name, size in ((3, "lo", lo_n), (1, "core", 2), (0, "y", y_n), (2, "hi", hi_n)):
        steps = [small] + [swap(small, name, step, size) for step in range(1, size)]
        small = jnp.concatenate(steps, axis)
    small = small.astype(jnp.float32)

    def gain_of(values):
        for at, axis in ((y_at, 0), (core_at, 1), (hi_at, 2), (lo_at, 3)):
            values = by_step(values, at, axis)
        return values.transpose(2, 0, 1, 3, 4).reshape(width)

    gain_one = gain_of(small[..., :own_rows])
    gain_two = gain_of(small[..., own_rows : 2 * own_rows])
    segments = small[..., 2 * own_rows : 2 * own_rows + rows]
    segments = segments.reshape(y_n, 2, hi_n, lo_n, seq_b, local_len)
    segments = by_step(segments, hi_at, 2).transpose(0, 1, 4, 2, 3, 5)
    steps = [(hi_at - step) % hi_n for step in range(hi_n)]
    segments = jnp.concatenate(
        [lax.dynamic_index_in_dim(segments, step, 3) for step in steps], 3
    )
    seqs = y_n * 2 * seq_b
    queries_len = lo_n * local_len
    key_segments = segments.reshape(seqs, seq_len)
    query_segments = key_segments[:, :queries_len]
    lo_place = lo_at ^ jnp.arange(lo_n)
    inner = (lo_place[:, None] * local_len + jnp.arange(local_len)[None, :]).reshape(queries_len)
    query_place = hi_at * queries_len + inner
    key_place = (hi_at - jnp.arange(hi_n)) % hi_n
    key_place = (key_place[:, None] * queries_len + inner[None, :]).reshape(seq_len)
    masks = (
        key_segments.reshape(seqs, 1, seq_len),
        key_place.reshape(1, seq_len),
        query_segments.reshape(seqs, queries_len, 1),
        query_place.reshape(queries_len, 1),
    )
    place_shape = (lo_n, local_len)
    frequency = ROPE_BASE ** (-(jnp.arange(HALF, dtype=jnp.float32) * 2.0 / HEAD_DIM))
    angles = query_place.astype(jnp.float32)[:, None] * frequency[None, :]
    cosine, sine_table = jnp.cos(angles), jnp.sin(angles)

    heads_full = everywhere(first_group)
    out_window, qkv_window = [(0, OUT_COLS)], [(OUT_COLS, QKV_COLS)]
    hidden = shuffle(hidden_in.reshape(rows, width), order)
    cotangent = shuffle(grad_output.reshape(rows, width), order)
    hidden_all, gate_group, up_group = spread_and_gather(
        after(hidden, first_group, gain_one, cotangent, *masks, cosine, sine_table),
        [widen(gate_weight), widen(up_weight)],
        0,
    )
    gate_full = everywhere(gate_group)
    source = hidden.astype(jnp.float32)
    inv_one = lax.rsqrt(jnp.mean(source * source, -1, keepdims=True) + EPSILON)
    normed_one = source * inv_one

    slots = (y_n, lo_n, 2, seq_b, local_len)
    packed = 2 * seq_b * 2 * HEAD_DIM

    def over_slots(cols):
        return pl.BlockSpec((1, 2, seq_b, local_len, cols), lambda lo: (lo, 0, 0, 0, 0))

    def slot_table():
        return pl.BlockSpec((1, local_len, HALF), lambda chip: (chip % lo_n, 0, 0))

    def slot_rows(cols):
        return pl.BlockSpec((2 * rows, cols), lambda lo: (lo, 0))

    normed_low, queries, key_value = pl.pallas_call(
        project_kernel,
        grid=(CHIPS,),
        in_specs=[
            slot_rows(width),
            pl.BlockSpec((1, width), lambda lo: (0, 0)),
            pl.BlockSpec(heads_full.shape, lambda lo: (0, 0), pipeline_mode=pl.Buffered(1)),
            slot_table(),
            slot_table(),
        ],
        out_specs=[
            slot_rows(width),
            slot_rows(query_cols),
            pl.BlockSpec((local_len, packed), lambda lo: (lo, 0)),
        ],
        out_shape=[
            jax.ShapeDtypeStruct((tokens, width), jnp.bfloat16),
            jax.ShapeDtypeStruct((tokens, query_cols), jnp.bfloat16),
            jax.ShapeDtypeStruct((CHIPS * local_len, packed), jnp.bfloat16),
        ],
        compiler_params=params(),
        name="project",
    )(
        hidden_all.reshape(tokens, width),
        gain_one.reshape(1, width),
        heads_full,
        cosine.reshape(place_shape + (HALF,)),
        sine_table.reshape(place_shape + (HALF,)),
    )
    queries = queries.reshape(slots + (query_cols,))
    cotangent_all, down_group, others = spread_and_gather(
        cotangent, [widen(down_weight)], 7, (key_value,)
    )
    cotangent_all = cotangent_all.reshape(tokens, width)
    up_full = everywhere(up_group)
    down_full = everywhere(down_group)


    def of_seq(at):
        return at // (2 * seq_b), 0, at // seq_b % 2, at % seq_b, 0, 0

    def per_seq(cols):
        return pl.BlockSpec((1, lo_n, 1, 1, local_len, cols), of_seq)

    own_spec = pl.BlockSpec((queries_len, packed), lambda at: (at // (2 * seq_b), 0))
    others_spec = pl.BlockSpec(
        (hi_n - 1, queries_len, packed), lambda at: (0, at // (2 * seq_b), 0)
    )
    pair_scratch = pltpu.VMEM((seq_len, 2 * HEAD_DIM), jnp.bfloat16)
    log_spec = pl.BlockSpec((1, REPEAT, queries_len), lambda at: (at, 0, 0))
    mask_specs = [
        pl.BlockSpec((1, 1, seq_len), lambda at: (at, 0, 0)),
        pl.BlockSpec((1, seq_len), lambda at: (0, 0)),
        pl.BlockSpec((1, queries_len, 1), lambda at: (at, 0, 0)),
        pl.BlockSpec((queries_len, 1), lambda at: (0, 0)),
    ]
    mixed_rows, log_total = pl.pallas_call(
        attend_kernel,
        grid=(seqs,),
        in_specs=[per_seq(query_cols), own_spec, others_spec] + mask_specs,
        out_specs=[per_seq(OUT_COLS), log_spec],
        out_shape=[
            jax.ShapeDtypeStruct(slots + (OUT_COLS,), jnp.bfloat16),
            jax.ShapeDtypeStruct((seqs, REPEAT, queries_len), jnp.float32),
        ],
        scratch_shapes=[pltpu.VMEM((seq_len, queries_len), jnp.float32), pair_scratch],
        compiler_params=params(),
        name="attend",
    )(queries, key_value, others, *masks)
    mixed_rows = mixed_rows.reshape(tokens, OUT_COLS)
    middle = source + dot_scatter([mixed_rows], [heads_full], 1, windows=out_window)

    inv_two = lax.rsqrt(jnp.mean(middle * middle, -1, keepdims=True) + EPSILON)
    normed_two = middle * inv_two
    normed_mid, gate_value, up_value, active = gather_dot(
        (normed_two * gain_two).astype(jnp.bfloat16),
        [gate_full, up_full],
        (jnp.float32, jnp.float32, jnp.bfloat16),
        2,
        gated=True,
    )
    normed_mid = normed_mid.reshape(tokens, width)
    gate_value = gate_value.reshape(tokens, -1)
    up_value = up_value.reshape(tokens, -1)
    active = active.reshape(tokens, -1)
    (down_product,) = products(cotangent_all, [active])
    down_summed = sum_along(down_product)
    grad_active = dot(after(cotangent_all, down_product), down_full)
    sigmoid_gate = jax.nn.sigmoid(gate_value)
    grad_gate = (
        grad_active * up_value * sigmoid_gate * (1.0 + gate_value * (1.0 - sigmoid_gate))
    ).astype(jnp.bfloat16)
    grad_up = (grad_active * jax.nn.silu(gate_value)).astype(jnp.bfloat16)
    gate_product, up_product = products(normed_mid, [grad_gate, grad_up])
    gate_summed = sum_along(gate_product)
    grad_norm_mid = dot_scatter(
        [after(grad_gate, gate_product), grad_up], [gate_full, up_full], 4
    )
    scaled_two = grad_norm_mid * gain_two
    grad_middle = cotangent.astype(jnp.float32) + inv_two * (
        scaled_two - normed_two * jnp.mean(scaled_two * normed_two, -1, keepdims=True)
    )

    def finish(back):
        return jnp.swapaxes(back, 0, 1).astype(jnp.float32)

    grad_branch, grad_mixed = gather_dot(
        grad_middle.astype(jnp.bfloat16), [heads_full], (jnp.bfloat16,), 5, windows=out_window
    )
    grad_branch = grad_branch.reshape(tokens, width)
    up_summed = sum_along(up_product)
    both_back = from_group(
        jnp.concatenate([after(down_summed, grad_mixed), after(gate_summed, grad_mixed)], 1)
    )
    down_back, gate_back = both_back[..., : ff_pad // SPLIT], both_back[..., ff_pad // SPLIT :]

    def finish_mlp(back):
        return finish(back).reshape(own_rows, ff_pad)[:, :ff_width]

    down_grads, gate_grads = finish_mlp(down_back), finish_mlp(gate_back)

    grad_queries, grad_key_value = pl.pallas_call(
        attend_back_kernel,
        grid=(seqs,),
        in_specs=[per_seq(query_cols), own_spec, others_spec, per_seq(OUT_COLS), log_spec]
        + mask_specs
        + [pl.BlockSpec((HALF, queries_len), lambda at: (0, 0))] * 2,
        out_specs=[
            per_seq(query_cols),
            pl.BlockSpec((hi_n, queries_len, packed), lambda at: (0, at // (2 * seq_b), 0)),
        ],
        out_shape=[
            jax.ShapeDtypeStruct(slots + (query_cols,), jnp.bfloat16),
            jax.ShapeDtypeStruct((hi_n, CHIPS * local_len, packed), jnp.bfloat16),
        ],
        scratch_shapes=[pltpu.VMEM((seq_len, queries_len), jnp.float32), pair_scratch],
        compiler_params=params(),
        name="attend_back",
    )(
        queries, key_value, others, grad_mixed.reshape(slots + (OUT_COLS,)), log_total, *masks,
        cosine.T, sine_table.T,
    )
    final, others, out_product = dot_scatter(
        [after(active, both_back)],
        [down_full],
        3,
        (grad_key_value,),
        host=([grad_branch], (0,), [mixed_rows]),
    )
    out_summed = sum_along(after(out_product, up_summed))
    up_back = from_group(after(up_summed, final))
    up_grads = finish_mlp(up_back)
    result = shuffle((middle + final).astype(jnp.bfloat16), back)
    flat = (CHIPS, 2, seq_b, local_len)
    grad_qkv = pl.pallas_call(
        unrotate_kernel,
        grid=(CHIPS,),
        in_specs=[
            over_slots(query_cols),
            pl.BlockSpec((1, local_len, packed), lambda chip: (0, chip, 0)),
            pl.BlockSpec((hi_n - 1, local_len, packed), lambda chip: (0, chip, 0)),
            slot_table(),
            slot_table(),
        ],
        out_specs=over_slots(512),
        out_shape=jax.ShapeDtypeStruct(flat + (512,), jnp.bfloat16),
        compiler_params=params(),
        name="unrotate",
    )(
        after(grad_queries, final).reshape(flat + (query_cols,)),
        grad_key_value,
        others,
        cosine.reshape(place_shape + (HALF,)),
        sine_table.reshape(place_shape + (HALF,)),
    ).reshape(tokens, 512)
    (qkv_product,) = products(normed_low, [grad_qkv])
    qkv_summed = sum_along(qkv_product)
    grad_norm_one = dot_scatter(
        [after(grad_qkv, qkv_product, out_summed)], [heads_full], 6, windows=qkv_window
    )
    grad_norm_one = after(grad_norm_one, up_back)
    scaled_one = grad_norm_one * gain_one
    grad_input = grad_middle + inv_one * (
        scaled_one - normed_one * jnp.mean(scaled_one * normed_one, -1, keepdims=True)
    )
    head_grads = finish(from_group(jnp.concatenate([out_summed, qkv_summed], 1)))
    key_at = OUT_COLS + query_cols

    def columns(start, count):
        return head_grads[..., start : start + count].reshape(own_rows, -1)

    grad_query = columns(OUT_COLS, query_cols)
    grad_key = columns(key_at, HEAD_DIM)
    grad_value = columns(key_at + HEAD_DIM, HEAD_DIM)

    def gain_grad(gain, pairs):
        total = sum(jnp.sum(weight.astype(jnp.float32) * grad, 1) for weight, grad in pairs)
        return total / gain.astype(jnp.float32)

    attn_gain_grad = gain_grad(
        attn_gain,
        [(query_weight, grad_query), (key_weight, grad_key), (value_weight, grad_value)],
    )
    mlp_gain_grad = gain_grad(mlp_gain, [(gate_weight, gate_grads), (up_weight, up_grads)])
    return (
        result.reshape(seq_b, local_len, width),
        shuffle(grad_input, back).reshape(seq_b, local_len, width),
        attn_gain_grad,
        grad_query,
        grad_key,
        grad_value,
        columns(0, query_cols),
        mlp_gain_grad,
        gate_grads,
        up_grads,
        down_grads,
    )


def solution(mesh):
    y_n = mesh.shape["batch"] // 2
    lo_n = CHIPS // y_n
    hi_n = mesh.shape["seq"] // lo_n
    fine = Mesh(mesh.devices.reshape(y_n, 2, hi_n, lo_n), EVERY)
    token = P(("y", "core"), ("hi", "lo"), None)
    vector = P(EVERY)
    matrix = P(EVERY, None)
    in_specs = (
        token, vector, matrix, matrix, matrix, matrix, vector, matrix, matrix, matrix,
        P(("y", "core"), None), token,
    )
    out_specs = (
        token, token, vector, matrix, matrix, matrix, matrix, vector, matrix, matrix, matrix,
    )

    def run(*arrays):
        return shards((y_n, hi_n, lo_n), *arrays)

    return jax.shard_map(run, mesh=fine, in_specs=in_specs, out_specs=out_specs, check_vma=False)
```
